128 devices in a mesh: grp: 4 (over y), col: 32 (over x, z, core).
Axes of the slice: x: 4, y: 4, z: 4, core: 2. Of those that a mesh axis runs over, the one named last changes fastest.
Arguments:
- blocks: bfloat16 [24576, 32, 1024], P(('grp', 'col'))
- i_index: int32 [24576], P(('grp', 'col')), may hold values from 0 to 63
- j_index: int32 [24576], P(('grp', 'col')), may hold values from 0 to 63
- k_index: int32 [24576], P(('grp', 'col')), may hold values from 0 to 15
- block_count: int32 [128], P(('grp', 'col')), may hold values from 24 to 192, as said below
- b_factor: float32 [65536, 256], P(('grp', 'col'))
- c_factor: float32 [16384, 256], P(('grp', 'col'))
Outputs:
- a_update: float32 [8192, 256], P(('grp', 'col'))
- b_update: float32 [65536, 256], P(('grp', 'col'))
The draws below stay inside these ranges and needn't reach their ends.
Inputs may be any that keep to these rules, and one draw needn't show every extreme that they name: block_count[d] is the number of live slots of device d = 32 * (grp index) + (col index): its slots d * 192 to d * 192 + block_count[d] - 1; every other slot is ignored. Some device has exactly 192 live slots.
All inputs are finite; a program needn't handle non-finite values.
Results may differ from the reference program's by a relative error of at most 0.005.
The reference program's roundings to bfloat16 on the way count: a program that leaves them out, or rounds other values in their place, can miss the bound.
Values may be sent and summed in bfloat16 or wider, within the bound.
No kernel may reach another device: no remote copies, remote signals or barrier semaphores. Data moves between devices by JAX's collectives and lax.ppermute only.
A program may use at most 128 MiB of HBM per device.

```python
import math
import jax
import jax.numpy as jnp
from jax import lax

RANK = 256
EDGE = 32
CAP = 192
B_DEV = 16
C_DEV = 4
COLUMNS = 32
SHARDS = 128
BLOCKS = 24576
IBOX = 64
JBOX = 64
KBOX = 16
IROWS = 8192
JROWS = 65536
KROWS = 16384


def draw_blocks(key, part):
    first = jax.random.fold_in(jax.random.fold_in(key, 11), 0)
    block_shape = (BLOCKS, EDGE, EDGE * EDGE)
    base_scale = 0.5 * math.sqrt(JROWS * KROWS * IROWS / (0.31 * BLOCKS * EDGE ** 3))
    position = (jnp.arange(BLOCKS) // CAP).astype(jnp.float32) / max(SHARDS - 1, 1)
    rising = jnp.sqrt(jnp.power(5.0, position) / 2.5)
    values = jnp.clip(jax.random.normal(first, block_shape, jnp.float32), -6.0, 6.0)
    return (values * (base_scale * rising)[:, None, None]).astype(jnp.bfloat16)


def mixed_factor(key, rows):
    subkeys = jax.random.split(key, 3)
    noise = jnp.clip(jax.random.normal(subkeys[0], (rows, RANK), jnp.float32), -6.0, 6.0)
    first_mix = jax.random.uniform(subkeys[1], (RANK,), jnp.float32, 0.6, 1.0)
    second_mix = jax.random.uniform(subkeys[2], (RANK,), jnp.float32, 0.6, 1.0)
    mixed = 0.6 * noise + first_mix[None, :] * jnp.roll(noise, -1, axis=1) + second_mix[None, :] * jnp.roll(noise, -5, axis=1)
    ramp = jnp.sqrt(1.0 + 2.0 * jnp.arange(rows).astype(jnp.float32) / max(rows - 1, 1))
    return mixed * ramp[:, None] / math.sqrt(3.28 * rows)


def draw_b_factor(key, part):
    return mixed_factor(jax.random.fold_in(key, 3), JROWS)


def draw_c_factor(key, part):
    return mixed_factor(jax.random.fold_in(key, 7), KROWS)


def draw_block_count(key, part):
    first, second = jax.random.split(jax.random.fold_in(key, 5))
    counts = jax.random.randint(first, (SHARDS,), CAP // 8, CAP // 2 + 1)
    chosen = jax.random.randint(second, (), 0, SHARDS)
    return jnp.where(jnp.arange(SHARDS) == chosen, CAP, counts).astype(jnp.int32)


def with_ends(values, own_key, least, high):
    shape = values.shape
    index_at = [jax.random.randint(jax.random.fold_in(own_key, axis), (), 0, shape[axis]) for axis in range(len(shape))]
    values = values.at[tuple(index_at)].set(least)
    longest = shape.index(max(shape))
    index_at[longest] = (index_at[longest] + 1) % shape[longest]
    return values.at[tuple(index_at)].set(high)


def setup_inputs(seed: int = 0) -> dict:
    key_of = jax.random.split(jax.random.key(seed), 8)
    blocks = draw_blocks(jax.random.fold_in(key_of[7], 71), 0)
    i_index = with_ends(jax.random.randint(key_of[1], (BLOCKS,), 0, IBOX), jax.random.fold_in(key_of[1], 1), 0, IBOX - 1).astype(jnp.int32)
    j_index = with_ends(jax.random.randint(key_of[2], (BLOCKS,), 0, JBOX), jax.random.fold_in(key_of[2], 1), 0, JBOX - 1).astype(jnp.int32)
    k_index = with_ends(jax.random.randint(key_of[3], (BLOCKS,), 0, KBOX), jax.random.fold_in(key_of[3], 1), 0, KBOX - 1).astype(jnp.int32)
    block_count = draw_block_count(jax.random.fold_in(key_of[7], 71), 0)
    b_factor = draw_b_factor(jax.random.fold_in(key_of[7], 71), 0)
    c_factor = draw_c_factor(jax.random.fold_in(key_of[7], 71), 0)
    return dict(blocks=blocks, i_index=i_index, j_index=j_index, k_index=k_index, block_count=block_count, b_factor=b_factor, c_factor=c_factor)


def solve_rows(gram, right_side):
    factor_low = lax.linalg.cholesky(gram)
    halfway = lax.linalg.triangular_solve(factor_low, right_side, left_side=False, lower=True, transpose_a=True)
    return lax.linalg.triangular_solve(factor_low, halfway, left_side=False, lower=True, transpose_a=False)

def accumulate(blocks, left_table, left_global, tail_table, tail_global, target_global, live_mask, targets, first_mode):
    steps_total = blocks.shape[0] // 64
    edge_size = blocks.shape[1]
    rank_width = left_table.shape[2]

    def one_step(running, inputs):
        tensor_group, left_idx, tail_idx, target_idx, alive_row = inputs
        left_rows = left_table[left_idx].astype(jnp.float32)
        tail_rows = tail_table[tail_idx].astype(jnp.float32)
        product = (left_rows[:, :, None, :] * tail_rows[:, None, :, :]).astype(jnp.bfloat16)
        product = lax.optimization_barrier(product).astype(jnp.float32)
        tensor_wide = tensor_group.astype(jnp.float32)
        if first_mode:
            result = jnp.einsum('bim,bmr->bir', tensor_wide, product.reshape(64, edge_size * edge_size, rank_width), precision=lax.Precision.HIGHEST)
        else:
            result = jnp.einsum('bijk,bikr->bjr', tensor_wide.reshape(64, edge_size, edge_size, edge_size), product, precision=lax.Precision.HIGHEST)
        result = result * alive_row[:, None, None]
        return (running.at[target_idx].add(result), None)
    inputs = (blocks.reshape(steps_total, 64, edge_size, edge_size * edge_size), left_global.reshape(steps_total, 64), tail_global.reshape(steps_total, 64), target_global.reshape(steps_total, 64), live_mask.reshape(steps_total, 64))
    start_value = jnp.zeros((targets, edge_size, rank_width), jnp.float32)
    running, _ = lax.scan(one_step, start_value, inputs)
    return running.reshape(targets * edge_size, rank_width)

def reference(blocks, i_index, j_index, k_index, block_count, b_factor, c_factor):
    highest = lax.Precision.HIGHEST
    slot_ids = jnp.arange(BLOCKS, dtype=jnp.int32)
    device = slot_ids // CAP
    group_index = device // COLUMNS
    column = device % COLUMNS
    live_mask = (slot_ids % CAP < block_count[device]).astype(jnp.float32)
    i_global = (group_index * IBOX + i_index).astype(jnp.int32)
    j_global = ((j_index // B_DEV * COLUMNS + column) * B_DEV + j_index % B_DEV).astype(jnp.int32)
    k_global = ((k_index // C_DEV * COLUMNS + column) * C_DEV + k_index % C_DEV).astype(jnp.int32)
    gram_second = jnp.dot(b_factor.T, b_factor, precision=highest)
    gram_third = jnp.dot(c_factor.T, c_factor, precision=highest)
    b_table = b_factor.astype(jnp.bfloat16).reshape(JROWS // EDGE, EDGE, RANK)
    c_table = c_factor.astype(jnp.bfloat16).reshape(KROWS // EDGE, EDGE, RANK)
    mode_one = accumulate(blocks, b_table, j_global, c_table, k_global, i_global, live_mask, IROWS // EDGE, True)
    a_update = solve_rows(gram_second * gram_third, mode_one)
    gram_first = jnp.dot(a_update.T, a_update, precision=highest)
    col_norm = jnp.sqrt(jnp.diagonal(gram_first) + 1e-06)
    a_table = (a_update / col_norm[None, :]).astype(jnp.bfloat16).reshape(IROWS // EDGE, EDGE, RANK)
    mode_two = accumulate(blocks, a_table, i_global, c_table, k_global, j_global, live_mask, JROWS // EDGE, False)
    gram_two = gram_first / (col_norm[:, None] * col_norm[None, :]) * gram_third
    b_update = solve_rows(gram_two, mode_two)
    return (a_update, b_update)
```

```python
import jax
import jax.numpy as jnp
from jax import lax
from jax.experimental import pallas as pl
from jax.experimental.pallas import tpu as pltpu
from jax.sharding import Mesh
from jax.sharding import PartitionSpec as P

EDGE = 32
STEP = 16
UNROLL = 8
VMEM_BYTES = 48 << 20
ALL = ("grp", "x", "z", "core")
PLANE = ("x", "z")
F32 = jnp.float32
BF16 = jnp.bfloat16
HIGHEST = lax.Precision.HIGHEST


def invert_four(p):
    inv_det = 1.0 / (p[0][0] * p[1][1] - p[0][1] * p[0][1])
    a00, a01, a11 = p[1][1] * inv_det, -p[0][1] * inv_det, p[0][0] * inv_det
    t00 = a00 * p[0][2] + a01 * p[1][2]
    t01 = a00 * p[0][3] + a01 * p[1][3]
    t10 = a01 * p[0][2] + a11 * p[1][2]
    t11 = a01 * p[0][3] + a11 * p[1][3]
    s00 = p[2][2] - (p[0][2] * t00 + p[1][2] * t10)
    s01 = p[2][3] - (p[0][2] * t01 + p[1][2] * t11)
    s11 = p[3][3] - (p[0][3] * t01 + p[1][3] * t11)
    inv_det = 1.0 / (s00 * s11 - s01 * s01)
    z00, z01, z11 = s11 * inv_det, -s01 * inv_det, s00 * inv_det
    u00, u01 = t00 * z00 + t01 * z01, t00 * z01 + t01 * z11
    u10, u11 = t10 * z00 + t11 * z01, t10 * z01 + t11 * z11
    x00 = a00 + (u00 * t00 + u01 * t01)
    x01 = a01 + (u00 * t10 + u01 * t11)
    x11 = a11 + (u10 * t10 + u11 * t11)
    return [
        [x00, x01, -u00, -u01],
        [x01, x11, -u10, -u11],
        [-u00, -u10, z00, z01],
        [-u01, -u11, z01, z11],
    ]


def invert_block(w):
    n = w.shape[0]
    row = lax.broadcasted_iota(jnp.int32, (n, n), 0)
    col = lax.broadcasted_iota(jnp.int32, (n, n), 1)
    for k in range(0, n, 4):
        cols = [jnp.broadcast_to(w[:, k + q : k + q + 1], (n, n)) for q in range(4)]
        rows = [w[k + q : k + q + 1, :] for q in range(4)]
        pivot = [[cols[b][k + a : k + a + 1, :] for b in range(4)] for a in range(4)]
        inv = invert_four(pivot)
        lane = col[0:1, :]
        fresh = []
        for a in range(4):
            value = (inv[a][0] * rows[0] + inv[a][1] * rows[1]) + (
                inv[a][2] * rows[2] + inv[a][3] * rows[3]
            )
            for b in range(4):
                value = jnp.where(lane == k + b, inv[a][b], value)
            fresh.append(value)
        in_cols = (col >= k) & (col < k + 4)
        in_rows = (row >= k) & (row < k + 4)
        base = jnp.where(in_cols, 0.0, w)
        update = (cols[0] * fresh[0] + cols[1] * fresh[1]) + (
            cols[2] * fresh[2] + cols[3] * fresh[3]
        )
        out = base - update
        for a in range(4):
            out = jnp.where(row == k + a, fresh[a], out)
        w = out
    return w


def inverse_kernel(turn, gram, out, work):
    n = gram.shape[0]
    width = 64

    @pl.when(turn[0] == 0)
    def _():
        out[...] = jnp.zeros_like(out)

    @pl.when(turn[0] != 0)
    def _():
        row = lax.broadcasted_iota(jnp.int32, (n, n), 0)
        col = lax.broadcasted_iota(jnp.int32, (n, n), 1)
        diag = jnp.where(row == col, gram[...], 0.0)
        scale_row = lax.rsqrt(jnp.sum(diag, axis=0, keepdims=True))
        scale_col = lax.rsqrt(jnp.sum(diag, axis=1, keepdims=True))
        work[...] = gram[...] * scale_row * scale_col
        for b in range(n // width):
            span = slice(b * width, (b + 1) * width)
            block = invert_block(work[span, span])
            rows = jnp.dot(block, work[span, :], precision=HIGHEST, preferred_element_type=F32)
            parts = [jnp.zeros((width, width), F32)] * (n // width)
            parts[b] = block
            padded = jnp.concatenate(parts, axis=1)
            in_block = (col >= b * width) & (col < (b + 1) * width)
            rows = jnp.where(in_block[0:width], padded, rows)
            left = work[:, span]
            left_row = row[:, 0:width]
            left = jnp.where((left_row >= b * width) & (left_row < (b + 1) * width), 0.0, left)
            base = jnp.where(in_block, 0.0, work[...])
            work[...] = base - jnp.dot(left, rows, precision=HIGHEST, preferred_element_type=F32)
            work[span, :] = rows
        out[...] = work[...] * scale_row * scale_col


def inverse_of(turn, gram):
    n = gram.shape[0]
    return pl.pallas_call(
        inverse_kernel,
        out_shape=jax.ShapeDtypeStruct((n, n), F32),
        in_specs=[
            pl.BlockSpec(memory_space=pltpu.SMEM),
            pl.BlockSpec(memory_space=pltpu.VMEM),
        ],
        out_specs=pl.BlockSpec(memory_space=pltpu.VMEM),
        scratch_shapes=[pltpu.VMEM((n, n), F32)],
        compiler_params=pltpu.CompilerParams(vmem_limit_bytes=VMEM_BYTES),
        name="gram_inverse",
    )(turn, gram)


def block_rows(ref, start):
    return ref[pl.ds(pl.multiple_of(start, EDGE), EDGE), :]


def mode_one_kernel(meta, i_idx, j_idx, k_idx, blocks, table, keep, send, acc):
    step = pl.program_id(0)
    count, grp, core = meta[0], meta[1], meta[2]
    own = table.shape[0] // 4
    c_base = own - own // 5
    half = keep.shape[0]

    @pl.when(step == 0)
    def _():
        acc[...] = jnp.zeros_like(acc)

    for sub in range(STEP // UNROLL):
        base = step * STEP + sub * UNROLL

        @pl.when(base < count)
        def _():
            for u in range(UNROLL):
                s = base + u
                j, k, i = j_idx[s], k_idx[s], i_idx[s]
                b_start = ((grp - (j >> 4)) & 3) * own + (j & 15) * EDGE
                c_start = ((grp - (k >> 2)) & 3) * own + c_base + (k & 3) * EDGE
                b_rows = block_rows(table, b_start)
                c_rows = block_rows(table, c_start)
                product = (b_rows[:, None, :] * c_rows[None, :, :]).reshape(EDGE * EDGE, -1)
                result = jnp.dot(blocks[sub * UNROLL + u], product, preferred_element_type=F32)
                target = (((i >> 1) & 1) ^ core) * half + (i >> 2) * (2 * EDGE) + (i & 1) * EDGE
                target = jnp.where(s < count, target, 2 * half)
                acc[pl.ds(pl.multiple_of(target, EDGE), EDGE), :] += result

    @pl.when(step == pl.num_programs(0) - 1)
    def _():
        keep[...] = acc[0:half, :]
        send[...] = acc[half : 2 * half, :]


def mode_two_kernel(
    meta, i_idx, j_idx, k_idx, blocks, a_table, table, keep, send_1, send_2, send_3, acc, turned
):
    step = pl.program_id(0)
    count, grp, core = meta[0], meta[1], meta[2]
    own = table.shape[0] // 4
    c_base = own - own // 5
    half = a_table.shape[0] // 2
    part = keep.shape[0]

    @pl.when(step == 0)
    def _():
        acc[...] = jnp.zeros_like(acc)

    lane = lax.broadcasted_iota(jnp.int32, (8, 128), 1)
    low_half = lane < 64
    even_group = (lane // 32) % 2 == 0

    def turn(block, slot):
        wide = block.astype(F32)
        for jh in range(8):
            t = [wide[il * 8 : il * 8 + 8, jh * 128 : jh * 128 + 128] for il in range(4)]
            m = [None] * 4
            for il in range(2):
                m[il] = jnp.where(low_half, t[il], pltpu.roll(t[il + 2], 64, 1))
                m[il + 2] = jnp.where(low_half, pltpu.roll(t[il], 64, 1), t[il + 2])
            for q in (0, 2):
                j = jh * 4 + q
                turned[slot, j * 8 : j * 8 + 8, :] = jnp.where(
                    even_group, m[q], pltpu.roll(m[q + 1], 32, 1)
                )
                turned[slot, j * 8 + 8 : j * 8 + 16, :] = jnp.where(
                    even_group, pltpu.roll(m[q], 96, 1), m[q + 1]
                )
        return jnp.concatenate(
            [turned[slot, pl.ds(ih, EDGE, stride=8), :].astype(BF16) for ih in range(8)], axis=1
        )

    for sub in range(STEP // UNROLL):
        base = step * STEP + sub * UNROLL

        @pl.when(base < count)
        def _():
            for u in range(UNROLL):
                s = base + u
                j, k, i = j_idx[s], k_idx[s], i_idx[s]
                a_start = (((i >> 1) & 1) ^ core) * half + (i >> 2) * (2 * EDGE) + (i & 1) * EDGE
                c_start = ((grp - (k >> 2)) & 3) * own + c_base + (k & 3) * EDGE
                a_rows = block_rows(a_table, a_start)
                c_rows = block_rows(table, c_start)
                left = turn(blocks[sub * UNROLL + u], u)
                product = jnp.concatenate(
                    [
                        a_rows[il * 8 + ih : il * 8 + ih + 1, :] * c_rows
                        for ih in range(8)
                        for il in range(4)
                    ],
                    axis=0,
                )
                result = jnp.dot(left, product, preferred_element_type=F32)
                target = (((j >> 4) - grp) & 3) * part + (j & 15) * EDGE
                target = jnp.where(s < count, target, 4 * part)
                acc[pl.ds(pl.multiple_of(target, EDGE), EDGE), :] += result

    @pl.when(step == pl.num_programs(0) - 1)
    def _():
        keep[...] = acc[0:part, :]
        for q, ref in enumerate((send_1, send_2, send_3)):
            ref[...] = acc[(q + 1) * part : (q + 2) * part, :].astype(BF16)


def slot_block(step, meta, *_):
    return (jnp.minimum(step, jnp.maximum(meta[0] - 1, 0) // STEP), 0, 0)


def whole(shape):
    return pl.BlockSpec(shape, lambda step, *_: (0, 0))


def mode_one(meta, i_index, j_index, k_index, blocks, table):
    rank = table.shape[1]
    half = 32 * EDGE
    return pl.pallas_call(
        mode_one_kernel,
        out_shape=[jax.ShapeDtypeStruct((half, rank), F32)] * 2,
        grid_spec=pltpu.PrefetchScalarGridSpec(
            num_scalar_prefetch=4,
            grid=(blocks.shape[0] // STEP,),
            in_specs=[pl.BlockSpec((STEP,) + blocks.shape[1:], slot_block), whole(table.shape)],
            out_specs=[whole((half, rank))] * 2,
            scratch_shapes=[pltpu.VMEM((2 * half + EDGE, rank), F32)],
        ),
        compiler_params=pltpu.CompilerParams(vmem_limit_bytes=VMEM_BYTES),
        name="mode_one",
    )(meta, i_index, j_index, k_index, blocks, table)


def mode_two(meta, i_index, j_index, k_index, blocks, a_table, table):
    rank = table.shape[1]
    part = 16 * EDGE
    return pl.pallas_call(
        mode_two_kernel,
        out_shape=[jax.ShapeDtypeStruct((part, rank), F32)]
        + [jax.ShapeDtypeStruct((part, rank), BF16)] * 3,
        grid_spec=pltpu.PrefetchScalarGridSpec(
            num_scalar_prefetch=4,
            grid=(blocks.shape[0] // STEP,),
            in_specs=[
                pl.BlockSpec((STEP,) + blocks.shape[1:], slot_block),
                whole(a_table.shape),
                whole(table.shape),
            ],
            out_specs=[whole((part, rank))] * 4,
            scratch_shapes=[
                pltpu.VMEM((4 * part + EDGE, rank), F32),
                pltpu.VMEM((UNROLL, 8 * EDGE, 128), F32),
            ],
        ),
        compiler_params=pltpu.CompilerParams(vmem_limit_bytes=VMEM_BYTES),
        name="mode_two",
    )(meta, i_index, j_index, k_index, blocks, a_table, table)


def to_other_core(value):
    return lax.ppermute(value, "core", [(0, 1), (1, 0)])


def along_groups(value, shift):
    size = lax.axis_size("grp")
    return lax.ppermute(value, "grp", [(p, (p + shift) % size) for p in range(size)])


def exchange(value, axes):
    return lax.all_to_all(value, axes, 0, 0)


def on_device(blocks, i_index, j_index, k_index, block_count, b_factor, c_factor):
    rank = b_factor.shape[1]
    grp, core = lax.axis_index("grp"), lax.axis_index("core")
    plane = lax.axis_size(PLANE)
    devices = lax.axis_size(ALL)
    meta = jnp.stack([block_count[0], grp, core])
    other_count = to_other_core(block_count)
    lighter = (block_count < other_count) | ((block_count == other_count) & (core == 0))
    turn = lighter.astype(jnp.int32)

    own = jnp.concatenate([b_factor.astype(BF16), c_factor.astype(BF16)], axis=0)
    table = jnp.concatenate([own] + [along_groups(own, q) for q in (1, 2, 3)], axis=0)

    grams = jnp.concatenate(
        [
            jnp.dot(b_factor.T, b_factor, precision=HIGHEST),
            jnp.dot(c_factor.T, c_factor, precision=HIGHEST),
        ],
        axis=0,
    )
    pieces = exchange(grams.reshape(devices, -1, rank), ALL)
    piece = jnp.sum(pieces, axis=0)
    grams = exchange(jnp.broadcast_to(piece[None], (devices,) + piece.shape), ALL)
    grams = grams.reshape(2, rank, rank)
    gram_third = grams[1]

    keep, send = mode_one(meta, i_index, j_index, k_index, blocks, table)
    gram_one, keep = lax.optimization_barrier((grams[0] * gram_third, keep))
    inverse = inverse_of(turn, gram_one)
    inverse = jnp.where(lighter[0], inverse, to_other_core(inverse))
    pair_sum = (keep + to_other_core(send)).astype(BF16)
    arrived = exchange(pair_sum.reshape(plane, -1, rank), PLANE)
    a_update = jnp.dot(jnp.sum(arrived.astype(F32), axis=0), inverse, precision=HIGHEST)

    a_near = exchange(jnp.broadcast_to(a_update[None], (plane,) + a_update.shape), PLANE)
    a_near = a_near.reshape(-1, rank)
    a_far = to_other_core(a_near)
    a_rows = jnp.concatenate([a_near, a_far], axis=0)
    squares = jnp.sum(a_rows * a_rows, axis=0, keepdims=True)
    squares = squares + along_groups(squares, 1) + along_groups(squares, 2) + along_groups(squares, 3)
    col_norm = jnp.sqrt(squares + 1e-06)
    a_table = (a_rows / col_norm).astype(BF16)
    gram_own = jnp.dot(a_rows.T, a_rows, precision=HIGHEST)
    gram_first = (
        gram_own + along_groups(gram_own, 1) + along_groups(gram_own, 2) + along_groups(gram_own, 3)
    )

    keep, *sends = mode_two(meta, i_index, j_index, k_index, blocks, a_table, table)
    gram_two = gram_first / (col_norm.reshape(rank, 1) * col_norm) * gram_third
    gram_two, keep = lax.optimization_barrier((gram_two, keep))
    inverse = inverse_of(turn, gram_two)
    inverse = jnp.where(lighter[0], inverse, to_other_core(inverse))
    arrived = [along_groups(value, q + 1).astype(F32) for q, value in enumerate(sends)]
    own_two = keep + arrived[0] + arrived[1] + arrived[2]
    b_update = jnp.dot(own_two, inverse, precision=HIGHEST)
    return a_update, b_update


def solution(mesh):
    groups, columns = mesh.shape["grp"], mesh.shape["col"]
    side = round((columns // 2) ** 0.5)
    fine = Mesh(mesh.devices.reshape(groups, side, side, 2), ALL)
    row, flat = P(ALL, None), P(ALL)
    return jax.shard_map(
        on_device,
        mesh=fine,
        in_specs=(P(ALL, None, None), flat, flat, flat, flat, row, row),
        out_specs=(row, row),
        check_vma=False,
    )
```

```python
import jax
import jax.numpy as jnp
from jax import lax
from jax.experimental import pallas as pl
from jax.experimental.pallas import tpu as pltpu
from jax.sharding import Mesh
from jax.sharding import PartitionSpec as P

EDGE = 32
STEP = 16
UNROLL = 8
B_ROWS = 16 * EDGE
MODE_COST = pl.CostEstimate(flops=28_000_000_000, bytes_accessed=90_000_000, transcendentals=0)
INVERSE_COST = pl.CostEstimate(flops=16_000_000_000, bytes_accessed=50_000_000, transcendentals=0)
VMEM_BYTES = 48 << 20
ALL = ("grp", "x", "z", "core")
PLANE = ("x", "z")
F32 = jnp.float32
BF16 = jnp.bfloat16
HIGHEST = lax.Precision.HIGHEST


def invert_four(p):
    inv_det = 1.0 / (p[0][0] * p[1][1] - p[0][1] * p[0][1])
    a00, a01, a11 = p[1][1] * inv_det, -p[0][1] * inv_det, p[0][0] * inv_det
    t00 = a00 * p[0][2] + a01 * p[1][2]
    t01 = a00 * p[0][3] + a01 * p[1][3]
    t10 = a01 * p[0][2] + a11 * p[1][2]
    t11 = a01 * p[0][3] + a11 * p[1][3]
    s00 = p[2][2] - (p[0][2] * t00 + p[1][2] * t10)
    s01 = p[2][3] - (p[0][2] * t01 + p[1][2] * t11)
    s11 = p[3][3] - (p[0][3] * t01 + p[1][3] * t11)
    inv_det = 1.0 / (s00 * s11 - s01 * s01)
    z00, z01, z11 = s11 * inv_det, -s01 * inv_det, s00 * inv_det
    u00, u01 = t00 * z00 + t01 * z01, t00 * z01 + t01 * z11
    u10, u11 = t10 * z00 + t11 * z01, t10 * z01 + t11 * z11
    x00 = a00 + (u00 * t00 + u01 * t01)
    x01 = a01 + (u00 * t10 + u01 * t11)
    x11 = a11 + (u10 * t10 + u11 * t11)
    return [
        [x00, x01, -u00, -u01],
        [x01, x11, -u10, -u11],
        [-u00, -u10, z00, z01],
        [-u01, -u11, z01, z11],
    ]


def invert_block(w):
    n = w.shape[0]
    row = lax.broadcasted_iota(jnp.int32, (n, n), 0)
    col = lax.broadcasted_iota(jnp.int32, (n, n), 1)
    for k in range(0, n, 4):
        cols = [jnp.broadcast_to(w[:, k + q : k + q + 1], (n, n)) for q in range(4)]
        rows = [w[k + q : k + q + 1, :] for q in range(4)]
        pivot = [[cols[b][k + a : k + a + 1, :] for b in range(4)] for a in range(4)]
        inv = invert_four(pivot)
        lane = col[0:1, :]
        fresh = []
        for a in range(4):
            value = (inv[a][0] * rows[0] + inv[a][1] * rows[1]) + (
                inv[a][2] * rows[2] + inv[a][3] * rows[3]
            )
            for b in range(4):
                value = jnp.where(lane == k + b, inv[a][b], value)
            fresh.append(value)
        in_cols = (col >= k) & (col < k + 4)
        in_rows = (row >= k) & (row < k + 4)
        base = jnp.where(in_cols, 0.0, w)
        update = (cols[0] * fresh[0] + cols[1] * fresh[1]) + (
            cols[2] * fresh[2] + cols[3] * fresh[3]
        )
        out = base - update
        for a in range(4):
            out = jnp.where(row == k + a, fresh[a], out)
        w = out
    return w


def inverse_kernel(turn, gram, out, work):
    n = gram.shape[0]
    width = 64

    @pl.when(turn[0] == 0)
    def _():
        out[...] = jnp.zeros_like(out)

    @pl.when(turn[0] != 0)
    def _():
        row = lax.broadcasted_iota(jnp.int32, (n, n), 0)
        col = lax.broadcasted_iota(jnp.int32, (n, n), 1)
        diag = jnp.where(row == col, gram[...], 0.0)
        scale_row = lax.rsqrt(jnp.sum(diag, axis=0, keepdims=True))
        scale_col = lax.rsqrt(jnp.sum(diag, axis=1, keepdims=True))
        work[...] = gram[...] * scale_row * scale_col
        for b in range(n // width):
            span = slice(b * width, (b + 1) * width)
            block = invert_block(work[span, span])
            rows = jnp.dot(block, work[span, :], precision=HIGHEST, preferred_element_type=F32)
            parts = [jnp.zeros((width, width), F32)] * (n // width)
            parts[b] = block
            padded = jnp.concatenate(parts, axis=1)
            in_block = (col >= b * width) & (col < (b + 1) * width)
            rows = jnp.where(in_block[0:width], padded, rows)
            left = work[:, span]
            left_row = row[:, 0:width]
            left = jnp.where((left_row >= b * width) & (left_row < (b + 1) * width), 0.0, left)
            base = jnp.where(in_block, 0.0, work[...])
            work[...] = base - jnp.dot(left, rows, precision=HIGHEST, preferred_element_type=F32)
            work[span, :] = rows
        out[...] = work[...] * scale_row * scale_col


def inverse_of(turn, gram):
    n = gram.shape[0]
    return pl.pallas_call(
        inverse_kernel,
        out_shape=jax.ShapeDtypeStruct((n, n), F32),
        in_specs=[
            pl.BlockSpec(memory_space=pltpu.SMEM),
            pl.BlockSpec(memory_space=pltpu.VMEM),
        ],
        out_specs=pl.BlockSpec(memory_space=pltpu.VMEM),
        scratch_shapes=[pltpu.VMEM((n, n), F32)],
        compiler_params=pltpu.CompilerParams(vmem_limit_bytes=VMEM_BYTES),
        cost_estimate=INVERSE_COST,
        name="gram_inverse",
    )(turn, gram)


def prepare_kernel(b_factor, c_factor, own, grams):
    rank = b_factor.shape[1]
    rows = b_factor.shape[0]
    own[0:rows, :] = b_factor[...].astype(BF16)
    own[rows:, :] = c_factor[...].astype(BF16)
    for q, ref in enumerate((b_factor, c_factor)):
        grams[q * rank : (q + 1) * rank, :] = lax.dot_general(
            ref[...],
            ref[...],
            (((0,), (0,)), ((), ())),
            precision=HIGHEST,
            preferred_element_type=F32,
        )


def prepare(b_factor, c_factor):
    rank = b_factor.shape[1]
    rows = b_factor.shape[0] + c_factor.shape[0]
    return pl.pallas_call(
        prepare_kernel,
        out_shape=[
            jax.ShapeDtypeStruct((rows, rank), BF16),
            jax.ShapeDtypeStruct((2 * rank, rank), F32),
        ],
        compiler_params=pltpu.CompilerParams(vmem_limit_bytes=VMEM_BYTES),
        name="prepare",
    )(b_factor, c_factor)


def block_rows(ref, start):
    return ref[pl.ds(pl.multiple_of(start, EDGE), EDGE), :]


def mode_one_kernel(
    meta, i_idx, j_idx, k_idx, blocks, own_0, own_1, own_2, own_3, keep, send, acc, table
):
    step = pl.program_id(0)
    count, grp, core = meta[0], meta[1], meta[2]
    own = own_0.shape[0]
    c_base = B_ROWS
    half = keep.shape[0]

    @pl.when(step == 0)
    def _():
        acc[...] = jnp.zeros_like(acc)
        for q, ref in enumerate((own_0, own_1, own_2, own_3)):
            table[q * own : (q + 1) * own, :] = ref[...]

    for sub in range(STEP // UNROLL):
        base = step * STEP + sub * UNROLL

        @pl.when(base < count)
        def _():
            for u in range(UNROLL):
                s = base + u
                j, k, i = j_idx[s], k_idx[s], i_idx[s]
                b_start = ((grp - (j >> 4)) & 3) * own + (j & 15) * EDGE
                c_start = ((grp - (k >> 2)) & 3) * own + c_base + (k & 3) * EDGE
                b_rows = block_rows(table, b_start)
                c_rows = block_rows(table, c_start)
                product = (b_rows[:, None, :] * c_rows[None, :, :]).reshape(EDGE * EDGE, -1)
                result = jnp.dot(blocks[sub * UNROLL + u], product, preferred_element_type=F32)
                target = (((i >> 1) & 1) ^ core) * half + (i >> 2) * (2 * EDGE) + (i & 1) * EDGE
                target = jnp.where(s < count, target, 2 * half)
                acc[pl.ds(pl.multiple_of(target, EDGE), EDGE), :] += result

    @pl.when(step == pl.num_programs(0) - 1)
    def _():
        keep[...] = acc[0:half, :]
        send[...] = acc[half : 2 * half, :]


def mode_two_kernel(
    meta,
    i_idx,
    j_idx,
    k_idx,
    blocks,
    a_near,
    a_far,
    squares,
    own_0,
    own_1,
    own_2,
    own_3,
    keep,
    send_1,
    send_2,
    send_3,
    acc,
    turned,
    table,
    a_table,
):
    step = pl.program_id(0)
    count, grp, core = meta[0], meta[1], meta[2]
    own = own_0.shape[0]
    half = a_near.shape[0]
    part = keep.shape[0]

    @pl.when(step == 0)
    def _():
        acc[...] = jnp.zeros_like(acc)
        for q, ref in enumerate((own_0, own_1, own_2, own_3)):
            table[q * own : (q + 1) * own, :] = ref[...]
        col_norm = jnp.sqrt(squares[...] + 1e-06)
        a_table[0:half, :] = (a_near[...] / col_norm).astype(BF16)
        a_table[half : 2 * half, :] = (a_far[...] / col_norm).astype(BF16)

    lane = lax.broadcasted_iota(jnp.int32, (8, 128), 1)
    low_half = lane < 64
    even_group = (lane // 32) % 2 == 0

    def turn(block, slot):
        wide = block.astype(F32)
        for jh in range(8):
            t = [wide[il * 8 : il * 8 + 8, jh * 128 : jh * 128 + 128] for il in range(4)]
            m = [None] * 4
            for il in range(2):
                m[il] = jnp.where(low_half, t[il], pltpu.roll(t[il + 2], 64, 1))
                m[il + 2] = jnp.where(low_half, pltpu.roll(t[il], 64, 1), t[il + 2])
            for q in (0, 2):
                j = jh * 4 + q
                turned[slot, j * 8 : j * 8 + 8, :] = jnp.where(
                    even_group, m[q], pltpu.roll(m[q + 1], 32, 1)
                )
                turned[slot, j * 8 + 8 : j * 8 + 16, :] = jnp.where(
                    even_group, pltpu.roll(m[q], 96, 1), m[q + 1]
                )
        return jnp.concatenate(
            [turned[slot, pl.ds(ih, EDGE, stride=8), :].astype(BF16) for ih in range(8)], axis=1
        )

    for sub in range(STEP // UNROLL):
        base = step * STEP + sub * UNROLL

        @pl.when(base < count)
        def _():
            for u in range(UNROLL):
                s = base + u
                j, k, i = j_idx[s], k_idx[s], i_idx[s]
                a_start = (((i >> 1) & 1) ^ core) * half + (i >> 2) * (2 * EDGE) + (i & 1) * EDGE
                c_start = ((grp - (k >> 2)) & 3) * own + (k & 3) * EDGE
                a_rows = block_rows(a_table, a_start)
                c_rows = block_rows(table, c_start)
                left = turn(blocks[sub * UNROLL + u], u)
                product = jnp.concatenate(
                    [
                        a_rows[il * 8 + ih : il * 8 + ih + 1, :] * c_rows
                        for ih in range(8)
                        for il in range(4)
                    ],
                    axis=0,
                )
                result = jnp.dot(left, product, preferred_element_type=F32)
                target = (((j >> 4) - grp) & 3) * part + (j & 15) * EDGE
                target = jnp.where(s < count, target, 4 * part)
                acc[pl.ds(pl.multiple_of(target, EDGE), EDGE), :] += result

    @pl.when(step == pl.num_programs(0) - 1)
    def _():
        keep[...] = acc[0:part, :]
        for q, ref in enumerate((send_1, send_2, send_3)):
            ref[...] = acc[(q + 1) * part : (q + 2) * part, :].astype(BF16)


def slot_block(step, meta, *_):
    return (jnp.minimum(step, jnp.maximum(meta[0] - 1, 0) // STEP), 0, 0)


def whole(shape):
    return pl.BlockSpec(shape, lambda step, *_: (0, 0))


def mode_one(meta, i_index, j_index, k_index, blocks, pieces):
    rank = pieces[0].shape[1]
    half = 32 * EDGE
    return pl.pallas_call(
        mode_one_kernel,
        out_shape=[jax.ShapeDtypeStruct((half, rank), F32)] * 2,
        grid_spec=pltpu.PrefetchScalarGridSpec(
            num_scalar_prefetch=4,
            grid=(blocks.shape[0] // STEP,),
            in_specs=[pl.BlockSpec((STEP,) + blocks.shape[1:], slot_block)]
            + [whole(pieces[0].shape)] * 4,
            out_specs=[whole((half, rank))] * 2,
            scratch_shapes=[
                pltpu.VMEM((2 * half + EDGE, rank), F32),
                pltpu.VMEM((4 * pieces[0].shape[0], rank), BF16),
            ],
        ),
        compiler_params=pltpu.CompilerParams(vmem_limit_bytes=VMEM_BYTES),
        cost_estimate=MODE_COST,
        name="mode_one",
    )(meta, i_index, j_index, k_index, blocks, *pieces)


def mode_two(meta, i_index, j_index, k_index, blocks, a_near, a_far, squares, pieces):
    rank = a_near.shape[1]
    part = 16 * EDGE
    c_rows = pieces[0].shape[0] - B_ROWS
    return pl.pallas_call(
        mode_two_kernel,
        out_shape=[jax.ShapeDtypeStruct((part, rank), F32)]
        + [jax.ShapeDtypeStruct((part, rank), BF16)] * 3,
        grid_spec=pltpu.PrefetchScalarGridSpec(
            num_scalar_prefetch=4,
            grid=(blocks.shape[0] // STEP,),
            in_specs=[
                pl.BlockSpec((STEP,) + blocks.shape[1:], slot_block),
                whole(a_near.shape),
                whole(a_far.shape),
                whole(squares.shape),
            ]
            + [pl.BlockSpec((c_rows, rank), lambda step, *_: (B_ROWS // c_rows, 0))] * 4,
            out_specs=[whole((part, rank))] * 4,
            scratch_shapes=[
                pltpu.VMEM((4 * part + EDGE, rank), F32),
                pltpu.VMEM((UNROLL, 8 * EDGE, 128), F32),
                pltpu.VMEM((4 * c_rows, rank), BF16),
                pltpu.VMEM((2 * a_near.shape[0], rank), BF16),
            ],
        ),
        compiler_params=pltpu.CompilerParams(vmem_limit_bytes=VMEM_BYTES),
        cost_estimate=MODE_COST,
        name="mode_two",
    )(meta, i_index, j_index, k_index, blocks, a_near, a_far, squares, *pieces)


def to_other_core(value):
    return lax.ppermute(value, "core", [(0, 1), (1, 0)])


def along_groups(value, shift):
    size = lax.axis_size("grp")
    return lax.ppermute(value, "grp", [(p, (p + shift) % size) for p in range(size)])


def exchange(value, axes):
    return lax.all_to_all(value, axes, 0, 0)


def on_device(blocks, i_index, j_index, k_index, block_count, b_factor, c_factor):
    rank = b_factor.shape[1]
    grp, core = lax.axis_index("grp"), lax.axis_index("core")
    plane = lax.axis_size(PLANE)
    devices = lax.axis_size(ALL)
    meta = jnp.stack([block_count[0], grp, core])
    other_count = to_other_core(block_count)
    lighter = (block_count < other_count) | ((block_count == other_count) & (core == 0))
    turn = lighter.astype(jnp.int32)

    own, grams = prepare(b_factor, c_factor)
    pieces = [own] + [along_groups(own, q) for q in (1, 2, 3)]
    piece = jnp.sum(exchange(grams.reshape(devices, -1, rank), ALL), axis=0)
    piece, meta = lax.optimization_barrier((piece, meta))
    grams = exchange(jnp.broadcast_to(piece[None], (devices,) + piece.shape), ALL)

    keep, send = mode_one(meta, i_index, j_index, k_index, blocks, pieces)
    grams, keep, send = lax.optimization_barrier((grams, keep, send))
    pair_sum = (keep + to_other_core(send)).astype(BF16)
    arrived = exchange(pair_sum.reshape(plane, -1, rank), PLANE)
    sum_own = jnp.sum(arrived.astype(F32), axis=0)
    sum_near = exchange(jnp.broadcast_to(sum_own[None], (plane,) + sum_own.shape), PLANE)
    sum_near = sum_near.reshape(-1, rank)

    grams = grams.reshape(2, rank, rank)
    gram_third = grams[1]
    inverse = inverse_of(turn, grams[0] * gram_third)
    inverse = jnp.where(lighter[0], inverse, to_other_core(inverse))
    a_update = jnp.dot(sum_own, inverse, precision=HIGHEST)

    sum_far = to_other_core(sum_near)
    a_near = jnp.dot(sum_near, inverse, precision=HIGHEST)
    squares = jnp.sum(a_near * a_near, axis=0, keepdims=True)
    squares = squares + along_groups(squares, 1) + along_groups(squares, 2) + along_groups(squares, 3)
    squares = squares + to_other_core(squares)
    a_far = jnp.dot(sum_far, inverse, precision=HIGHEST)
    gram_near = jnp.dot(a_near.T, a_near, precision=HIGHEST)
    gram_plane = gram_near + to_other_core(gram_near)
    gram_parts = [gram_plane] + [along_groups(gram_plane, q) for q in (1, 2, 3)]

    keep, *sends = mode_two(
        meta, i_index, j_index, k_index, blocks, a_near, a_far, squares, pieces
    )
    gram_parts, keep = lax.optimization_barrier((gram_parts, keep))
    gram_first = gram_parts[0] + gram_parts[1] + gram_parts[2] + gram_parts[3]
    col_norm = jnp.sqrt(squares + 1e-06)
    gram_two = gram_first / (col_norm.reshape(rank, 1) * col_norm) * gram_third
    inverse = inverse_of(turn, gram_two)
    inverse, sends = lax.optimization_barrier((inverse, sends))
    inverse = jnp.where(lighter[0], inverse, to_other_core(inverse))
    arrived = [along_groups(value, q + 1).astype(F32) for q, value in enumerate(sends)]
    own_two = keep + arrived[0] + arrived[1] + arrived[2]
    b_update = jnp.dot(own_two, inverse, precision=HIGHEST)
    return a_update, b_update


def solution(mesh):
    groups, columns = mesh.shape["grp"], mesh.shape["col"]
    side = round((columns // 2) ** 0.5)
    fine = Mesh(mesh.devices.reshape(groups, side, side, 2), ALL)
    row, flat = P(ALL, None), P(ALL)
    return jax.shard_map(
        on_device,
        mesh=fine,
        in_specs=(P(ALL, None, None), flat, flat, flat, flat, row, row),
        out_specs=(row, row),
        check_vma=False,
    )
```

```python
import jax
import jax.numpy as jnp
from jax import lax
from jax.experimental import pallas as pl
from jax.experimental.pallas import tpu as pltpu
from jax.sharding import Mesh
from jax.sharding import PartitionSpec as P

EDGE = 32
GROUP = 8
B_ROWS = 16 * EDGE
MODE_COST = pl.CostEstimate(flops=15_000_000_000, bytes_accessed=48_000_000, transcendentals=0)
INVERSE_COST = pl.CostEstimate(flops=16_000_000_000, bytes_accessed=50_000_000, transcendentals=0)
VMEM_BYTES = 48 << 20
ALL = ("grp", "x", "z", "core")
PLANE = ("x", "z")
CHIPS = ("grp", "x", "z")
F32 = jnp.float32
BF16 = jnp.bfloat16
HIGHEST = lax.Precision.HIGHEST


def invert_four(p):
    inv_det = 1.0 / (p[0][0] * p[1][1] - p[0][1] * p[0][1])
    a00, a01, a11 = p[1][1] * inv_det, -p[0][1] * inv_det, p[0][0] * inv_det
    t00 = a00 * p[0][2] + a01 * p[1][2]
    t01 = a00 * p[0][3] + a01 * p[1][3]
    t10 = a01 * p[0][2] + a11 * p[1][2]
    t11 = a01 * p[0][3] + a11 * p[1][3]
    s00 = p[2][2] - (p[0][2] * t00 + p[1][2] * t10)
    s01 = p[2][3] - (p[0][2] * t01 + p[1][2] * t11)
    s11 = p[3][3] - (p[0][3] * t01 + p[1][3] * t11)
    inv_det = 1.0 / (s00 * s11 - s01 * s01)
    z00, z01, z11 = s11 * inv_det, -s01 * inv_det, s00 * inv_det
    u00, u01 = t00 * z00 + t01 * z01, t00 * z01 + t01 * z11
    u10, u11 = t10 * z00 + t11 * z01, t10 * z01 + t11 * z11
    x00 = a00 + (u00 * t00 + u01 * t01)
    x01 = a01 + (u00 * t10 + u01 * t11)
    x11 = a11 + (u10 * t10 + u11 * t11)
    return [
        [x00, x01, -u00, -u01],
        [x01, x11, -u10, -u11],
        [-u00, -u10, z00, z01],
        [-u01, -u11, z01, z11],
    ]


def invert_block(w):
    n = w.shape[0]
    row = lax.broadcasted_iota(jnp.int32, (n, n), 0)
    col = lax.broadcasted_iota(jnp.int32, (n, n), 1)
    for k in range(0, n, 4):
        cols = [jnp.broadcast_to(w[:, k + q : k + q + 1], (n, n)) for q in range(4)]
        rows = [w[k + q : k + q + 1, :] for q in range(4)]
        pivot = [[cols[b][k + a : k + a + 1, :] for b in range(4)] for a in range(4)]
        inv = invert_four(pivot)
        lane = col[0:1, :]
        fresh = []
        for a in range(4):
            value = (inv[a][0] * rows[0] + inv[a][1] * rows[1]) + (
                inv[a][2] * rows[2] + inv[a][3] * rows[3]
            )
            for b in range(4):
                value = jnp.where(lane == k + b, inv[a][b], value)
            fresh.append(value)
        in_cols = (col >= k) & (col < k + 4)
        in_rows = (row >= k) & (row < k + 4)
        base = jnp.where(in_cols, 0.0, w)
        update = (cols[0] * fresh[0] + cols[1] * fresh[1]) + (
            cols[2] * fresh[2] + cols[3] * fresh[3]
        )
        out = base - update
        for a in range(4):
            out = jnp.where(row == k + a, fresh[a], out)
        w = out
    return w


def tiles_of(matrix):
    across = matrix.shape[1] // 128
    return [
        (r * across + c, slice(r * 8, r * 8 + 8), slice(c * 128, c * 128 + 128))
        for r in range(matrix.shape[0] // 8)
        for c in range(across)
    ]


def invert(out, work):
    n = work.shape[0]
    width = 64
    row = lax.broadcasted_iota(jnp.int32, (n, n), 0)
    col = lax.broadcasted_iota(jnp.int32, (n, n), 1)
    diag = jnp.where(row == col, work[...], 0.0)
    scale_row = lax.rsqrt(jnp.sum(diag, axis=0, keepdims=True))
    scale_col = lax.rsqrt(jnp.sum(diag, axis=1, keepdims=True))
    work[...] = work[...] * scale_row * scale_col
    for b in range(n // width):
        span = slice(b * width, (b + 1) * width)
        block = invert_block(work[span, span])
        rows = jnp.dot(block, work[span, :], precision=HIGHEST, preferred_element_type=F32)
        parts = [jnp.zeros((width, width), F32)] * (n // width)
        parts[b] = block
        padded = jnp.concatenate(parts, axis=1)
        in_block = (col >= b * width) & (col < (b + 1) * width)
        rows = jnp.where(in_block[0:width], padded, rows)
        left = work[:, span]
        left_row = row[:, 0:width]
        left = jnp.where((left_row >= b * width) & (left_row < (b + 1) * width), 0.0, left)
        base = jnp.where(in_block, 0.0, work[...])
        work[...] = base - jnp.dot(left, rows, precision=HIGHEST, preferred_element_type=F32)
        work[span, :] = rows
    out[...] = work[...] * scale_row * scale_col


def first_inverse_kernel(meta, turn, near, far, out, work):
    @pl.when(turn[0] == 0)
    def _():
        out[...] = jnp.zeros_like(out)

    @pl.when(turn[0] != 0)
    def _():
        for t, rows, cols in tiles_of(work):
            work[rows, cols] = near[t] * far[t]
        invert(out, work)


def second_inverse_kernel(meta, turn, part_0, part_1, part_2, part_3, near, far, out, work):
    n = work.shape[0]

    @pl.when(turn[0] == 0)
    def _():
        out[...] = jnp.zeros_like(out)

    @pl.when(turn[0] != 0)
    def _():
        gram = (part_0[...] + part_1[...]) + (part_2[...] + part_3[...])
        row = lax.broadcasted_iota(jnp.int32, (n, n), 0)
        col = lax.broadcasted_iota(jnp.int32, (n, n), 1)
        diag = jnp.where(row == col, gram, 0.0)
        norm_row = jnp.sqrt(jnp.sum(diag, axis=0, keepdims=True) + 1e-06)
        norm_col = jnp.sqrt(jnp.sum(diag, axis=1, keepdims=True) + 1e-06)
        work[...] = gram / (norm_col * norm_row)
        third_is_near = meta[2] == 1
        for t, rows, cols in tiles_of(work):
            work[rows, cols] = work[rows, cols] * jnp.where(third_is_near, near[t], far[t])
        invert(out, work)


def inverse_of(kernel, name, meta, turn, *arrays):
    n = 256
    return pl.pallas_call(
        kernel,
        out_shape=jax.ShapeDtypeStruct((n, n), F32),
        in_specs=[pl.BlockSpec(memory_space=pltpu.SMEM)] * 2
        + [pl.BlockSpec(memory_space=pltpu.VMEM)] * len(arrays),
        out_specs=pl.BlockSpec(memory_space=pltpu.VMEM),
        scratch_shapes=[pltpu.VMEM((n, n), F32)],
        compiler_params=pltpu.CompilerParams(vmem_limit_bytes=VMEM_BYTES),
        cost_estimate=INVERSE_COST,
        name=name,
    )(meta, turn, *arrays)


def prepare_kernel(meta, b_factor, c_factor, own, gram_keep, gram_send):
    rows = b_factor.shape[0]
    core = meta[2]
    own[0:rows, :] = b_factor[...].astype(BF16)
    own[rows:, :] = c_factor[...].astype(BF16)
    for q, ref in enumerate((b_factor, c_factor)):
        gram = lax.dot_general(
            ref[...],
            ref[...],
            (((0,), (0,)), ((), ())),
            precision=HIGHEST,
            preferred_element_type=F32,
        )

        @pl.when(core == q)
        def _():
            for t, r, c in tiles_of(gram):
                gram_keep[t] = gram[r, c]

        @pl.when(core != q)
        def _():
            for t, r, c in tiles_of(gram):
                gram_send[t] = gram[r, c]


def prepare(meta, b_factor, c_factor):
    rank = b_factor.shape[1]
    rows = b_factor.shape[0] + c_factor.shape[0]
    tiles = jax.ShapeDtypeStruct((rank * rank // 1024, 8, 128), F32)
    return pl.pallas_call(
        prepare_kernel,
        out_shape=[jax.ShapeDtypeStruct((rows, rank), BF16), tiles, tiles],
        in_specs=[pl.BlockSpec(memory_space=pltpu.SMEM)]
        + [pl.BlockSpec(memory_space=pltpu.VMEM)] * 2,
        compiler_params=pltpu.CompilerParams(vmem_limit_bytes=VMEM_BYTES),
        name="prepare",
    )(meta, b_factor, c_factor)


def order_kernel(meta, i_idx, j_idx, order_one, order_two, ends):
    slots = i_idx.shape[0]
    grp, core = meta[1], meta[2]

    def clear(s, carry):
        order_one[s] = 0
        order_two[s] = 0
        return carry

    lax.fori_loop(0, slots, clear, 0, unroll=8)

    def place(s, carry):
        front_one, front_two = carry
        one = ((i_idx[s] >> 1) & 1) ^ core
        two = jnp.where((j_idx[s] >> 4) == grp, 0, 1)
        order_one[jnp.where(one == 1, front_one, slots - 1 - (s - front_one))] = s
        order_two[jnp.where(two == 1, front_two, slots - 1 - (s - front_two))] = s
        return front_one + one, front_two + two

    ends[0], ends[1] = lax.fori_loop(0, meta[0], place, (jnp.int32(0), jnp.int32(0)))


def order_slots(meta, i_index, j_index):
    table = jax.ShapeDtypeStruct(i_index.shape, jnp.int32)
    smem = pl.BlockSpec(memory_space=pltpu.SMEM)
    return pl.pallas_call(
        order_kernel,
        out_shape=[table, table, jax.ShapeDtypeStruct((2,), jnp.int32)],
        in_specs=[smem] * 3,
        out_specs=[smem] * 3,
        name="order_slots",
    )(meta, i_index, j_index)


def block_rows(ref, start):
    return ref[pl.ds(pl.multiple_of(start, EDGE), EDGE), :]


def copy_all(copies):
    for copy in copies:
        copy.start()
    return copies


def wait_all(copies):
    for copy in copies:
        copy.wait()


def for_each_group(first, count, order, blocks, buffer, sems, one_slot):
    slots = order.shape[0]
    groups = (count + GROUP - 1) // GROUP

    def slot_at(place):
        place = jnp.minimum(place, slots - 1)
        return order[place if first else slots - 1 - place]

    def copies(group):
        side = group & 1
        return [
            pltpu.make_async_copy(
                blocks.at[slot_at(group * GROUP + u)], buffer.at[side, u], sems.at[side, u]
            )
            for u in range(GROUP)
        ]

    @pl.when(groups > 0)
    def _():
        copy_all(copies(0))

    def one_group(group, carry):
        @pl.when(group + 1 < groups)
        def _():
            copy_all(copies(group + 1))

        wait_all(copies(group))
        for u in range(GROUP):
            place = group * GROUP + u
            one_slot(buffer[group & 1, u], u, slot_at(place), place < count)
        return carry

    lax.fori_loop(0, groups, one_group, 0)


def mode_one_kernel(
    first,
    meta,
    ends,
    order,
    i_idx,
    j_idx,
    k_idx,
    blocks,
    own_0,
    own_1,
    own_2,
    own_3,
    out,
    buffer,
    table,
    acc,
    sems,
    table_sems,
):
    grp = meta[1]
    own = own_0.shape[0]
    half = out.shape[0]
    count = ends[0] if first else meta[0] - ends[0]
    pieces = copy_all(
        [
            pltpu.make_async_copy(ref, table.at[pl.ds(q * own, own)], table_sems.at[q])
            for q, ref in enumerate((own_0, own_1, own_2, own_3))
        ]
    )
    acc[...] = jnp.zeros_like(acc)
    wait_all(pieces)

    def one_slot(block, u, s, live):
        j, k, i = j_idx[s], k_idx[s], i_idx[s]
        b_rows = block_rows(table, ((grp - (j >> 4)) & 3) * own + (j & 15) * EDGE)
        c_rows = block_rows(table, ((grp - (k >> 2)) & 3) * own + B_ROWS + (k & 3) * EDGE)
        product = (b_rows[:, None, :] * c_rows[None, :, :]).reshape(EDGE * EDGE, -1)
        result = jnp.dot(block, product, preferred_element_type=F32)
        target = jnp.where(live, (i >> 2) * (2 * EDGE) + (i & 1) * EDGE, half)
        acc[pl.ds(pl.multiple_of(target, EDGE), EDGE), :] += result

    for_each_group(first, count, order, blocks, buffer, sems, one_slot)
    out[...] = acc[0:half, :]


def turn_block(block, turned, u):
    lane = lax.broadcasted_iota(jnp.int32, (8, 128), 1)
    low_half = lane < 64
    even_group = (lane // 32) % 2 == 0
    wide = block.astype(F32)
    for jh in range(8):
        t = [wide[il * 8 : il * 8 + 8, jh * 128 : jh * 128 + 128] for il in range(4)]
        m = [None] * 4
        for il in range(2):
            m[il] = jnp.where(low_half, t[il], pltpu.roll(t[il + 2], 64, 1))
            m[il + 2] = jnp.where(low_half, pltpu.roll(t[il], 64, 1), t[il + 2])
        for q in (0, 2):
            j = jh * 4 + q
            turned[u, j * 8 : j * 8 + 8, :] = jnp.where(
                even_group, m[q], pltpu.roll(m[q + 1], 32, 1)
            )
            turned[u, j * 8 + 8 : j * 8 + 16, :] = jnp.where(
                even_group, pltpu.roll(m[q], 96, 1), m[q + 1]
            )
    return jnp.concatenate(
        [turned[u, pl.ds(ih, EDGE, stride=8), :].astype(BF16) for ih in range(8)], axis=1
    )


def mode_two_slots(
    first, meta, ends, order, i_idx, j_idx, k_idx, blocks, owns, a_table, scratch, part
):
    buffer, turned, table, acc, sems, table_sems = scratch
    grp, core = meta[1], meta[2]
    c_rows = table.shape[0] // 4
    half = a_table.shape[0] // 2
    count = ends[1] if first else meta[0] - ends[1]
    pieces = copy_all(
        [
            pltpu.make_async_copy(
                ref.at[pl.ds(B_ROWS, c_rows)],
                table.at[pl.ds(q * c_rows, c_rows)],
                table_sems.at[q],
            )
            for q, ref in enumerate(owns)
        ]
    )
    acc[...] = jnp.zeros_like(acc)
    wait_all(pieces)

    def one_slot(block, u, s, live):
        j, k, i = j_idx[s], k_idx[s], i_idx[s]
        a_rows = block_rows(
            a_table,
            (((i >> 1) & 1) ^ core) * half + (i >> 2) * (2 * EDGE) + (i & 1) * EDGE,
        )
        c_block = block_rows(table, ((grp - (k >> 2)) & 3) * c_rows + (k & 3) * EDGE)
        left = turn_block(block, turned, u)
        product = jnp.concatenate(
            [
                a_rows[il * 8 + ih : il * 8 + ih + 1, :] * c_block
                for ih in range(8)
                for il in range(4)
            ],
            axis=0,
        )
        result = jnp.dot(left, product, preferred_element_type=F32)
        target = (j & 15) * EDGE
        if first:
            target += (((j >> 4) - grp - 1) & 3) * part
        target = jnp.where(live, target, acc.shape[0] - EDGE)
        acc[pl.ds(pl.multiple_of(target, EDGE), EDGE), :] += result

    for_each_group(first, count, order, blocks, buffer, sems, one_slot)


def mode_two_others_kernel(
    meta,
    ends,
    order,
    i_idx,
    j_idx,
    k_idx,
    blocks,
    own_0,
    own_1,
    own_2,
    own_3,
    a_near,
    a_far,
    squares,
    send_1,
    send_2,
    send_3,
    a_table,
    *scratch,
):
    half = a_near.shape[0]
    part = send_1.shape[0]
    col_norm = jnp.sqrt(squares[...] + 1e-06)
    a_table[0:half, :] = (a_near[...] / col_norm).astype(BF16)
    a_table[half : 2 * half, :] = (a_far[...] / col_norm).astype(BF16)
    owns = (own_0, own_1, own_2, own_3)
    mode_two_slots(
        True, meta, ends, order, i_idx, j_idx, k_idx, blocks, owns, a_table, scratch, part
    )
    acc = scratch[3]
    for q, ref in enumerate((send_1, send_2, send_3)):
        ref[...] = acc[q * part : (q + 1) * part, :].astype(BF16)


def mode_two_own_kernel(
    meta,
    ends,
    order,
    i_idx,
    j_idx,
    k_idx,
    blocks,
    own_0,
    own_1,
    own_2,
    own_3,
    a_table,
    keep,
    *scratch,
):
    part = keep.shape[0]
    owns = (own_0, own_1, own_2, own_3)
    mode_two_slots(
        False, meta, ends, order, i_idx, j_idx, k_idx, blocks, owns, a_table, scratch, part
    )
    keep[...] = scratch[3][0:part, :]


def mode_call(kernel, name, scalars, in_place, resident, out_shape, scratch):
    smem, anywhere, vmem = (
        pl.BlockSpec(memory_space=pltpu.SMEM),
        pl.BlockSpec(memory_space=pl.ANY),
        pl.BlockSpec(memory_space=pltpu.VMEM),
    )
    blocks = in_place[0]
    buffer = pltpu.VMEM((2, GROUP) + blocks.shape[1:], blocks.dtype)
    return pl.pallas_call(
        kernel,
        out_shape=out_shape,
        in_specs=[smem] * len(scalars) + [anywhere] * len(in_place) + [vmem] * len(resident),
        out_specs=[vmem] * len(out_shape),
        scratch_shapes=[buffer]
        + scratch
        + [pltpu.SemaphoreType.DMA((2, GROUP)), pltpu.SemaphoreType.DMA((4,))],
        compiler_params=pltpu.CompilerParams(vmem_limit_bytes=VMEM_BYTES),
        cost_estimate=MODE_COST,
        name=name,
    )(*scalars, *in_place, *resident)


def mode_one(first, meta, ends, order, indices, blocks, pieces):
    own, rank = pieces[0].shape
    half = 32 * EDGE

    def kernel(*refs):
        mode_one_kernel(first, *refs)

    [out] = mode_call(
        kernel,
        "mode_one_other_core" if first else "mode_one_own_core",
        (meta, ends, order) + indices,
        [blocks] + pieces,
        [],
        [jax.ShapeDtypeStruct((half, rank), F32)],
        [pltpu.VMEM((4 * own, rank), BF16), pltpu.VMEM((half + EDGE, rank), F32)],
    )
    return out


def mode_two(first, meta, ends, order, indices, blocks, pieces, resident):
    rank = pieces[0].shape[1]
    part = 16 * EDGE
    c_rows = pieces[0].shape[0] - B_ROWS
    sent = jax.ShapeDtypeStruct((part, rank), BF16)
    if first:
        out_shape = [sent] * 3 + [jax.ShapeDtypeStruct((64 * EDGE, rank), BF16)]
    else:
        out_shape = [jax.ShapeDtypeStruct((part, rank), F32)]
    return mode_call(
        mode_two_others_kernel if first else mode_two_own_kernel,
        "mode_two_other_groups" if first else "mode_two_own_group",
        (meta, ends, order) + indices,
        [blocks] + pieces,
        resident,
        out_shape,
        [
            pltpu.VMEM((GROUP, 8 * EDGE, 128), F32),
            pltpu.VMEM((4 * c_rows, rank), BF16),
            pltpu.VMEM(((3 if first else 1) * part + EDGE, rank), F32),
        ],
    )


def to_other_core(value):
    return lax.ppermute(value, "core", [(0, 1), (1, 0)])


def along_groups(value, shift):
    size = lax.axis_size("grp")
    return lax.ppermute(value, "grp", [(p, (p + shift) % size) for p in range(size)])


def exchange(value, axes):
    return lax.all_to_all(value, axes, 0, 0)


def on_device(blocks, i_index, j_index, k_index, block_count, b_factor, c_factor):
    rank = b_factor.shape[1]
    grp, core = lax.axis_index("grp"), lax.axis_index("core")
    plane = lax.axis_size(PLANE)
    chips = lax.axis_size(CHIPS)
    indices = (i_index, j_index, k_index)
    meta = jnp.stack([block_count[0], grp, core])

    own, gram_keep, gram_send = prepare(meta, b_factor, c_factor)
    order_one, order_two, ends = order_slots(meta, i_index, j_index)
    gram_pair = gram_keep + to_other_core(gram_send)
    pieces = [own] + [along_groups(own, q) for q in (1, 2, 3)]
    gram_parts = exchange(gram_pair.reshape(chips, -1, 8, 128), CHIPS)
    send = mode_one(True, meta, ends, order_one, indices, blocks, pieces)
    piece = jnp.sum(gram_parts, axis=0)
    piece, send = lax.optimization_barrier((piece, send))
    spread = jnp.broadcast_to(piece[None], (chips,) + piece.shape)
    spread, order_one = lax.optimization_barrier((spread, order_one))
    gram_near = exchange(spread, CHIPS)
    keep = mode_one(False, meta, ends, order_one, indices, blocks, pieces)
    gram_near, keep = lax.optimization_barrier((gram_near, keep))
    gram_near = gram_near.reshape(-1, 8, 128)
    gram_far = to_other_core(gram_near)

    pair_sum = (keep + to_other_core(send)).astype(BF16)
    arrived = exchange(pair_sum.reshape(plane, -1, rank), PLANE)
    sum_own = jnp.sum(arrived.astype(F32), axis=0)
    sum_near = exchange(jnp.broadcast_to(sum_own[None], (plane,) + sum_own.shape), PLANE)
    sum_near = sum_near.reshape(-1, rank)

    other_count = to_other_core(block_count)
    lighter = (block_count < other_count) | ((block_count == other_count) & (core == 0))
    turn = lighter.astype(jnp.int32)
    inverse = inverse_of(first_inverse_kernel, "first_inverse", meta, turn, gram_near, gram_far)
    inverse = jnp.where(lighter[0], inverse, to_other_core(inverse))
    a_update = jnp.dot(sum_own, inverse, precision=HIGHEST)

    sum_far = to_other_core(sum_near)
    a_near = jnp.dot(sum_near, inverse, precision=HIGHEST)
    squares = jnp.sum(a_near * a_near, axis=0, keepdims=True)
    squares = squares + along_groups(squares, 1) + along_groups(squares, 2) + along_groups(squares, 3)
    squares = squares + to_other_core(squares)
    a_far = jnp.dot(sum_far, inverse, precision=HIGHEST)
    gram_core = jnp.dot(a_near.T, a_near, precision=HIGHEST)
    gram_plane = gram_core + to_other_core(gram_core)
    gram_parts = [gram_plane] + [along_groups(gram_plane, q) for q in (1, 2, 3)]

    *sends, a_table = mode_two(
        True, meta, ends, order_two, indices, blocks, pieces, [a_near, a_far, squares]
    )
    gram_parts, sends = lax.optimization_barrier((gram_parts, sends))
    inverse = inverse_of(
        second_inverse_kernel, "second_inverse", meta, turn, *gram_parts, gram_near, gram_far
    )
    inverse, sends, a_table = lax.optimization_barrier((inverse, sends, a_table))
    [keep] = mode_two(False, meta, ends, order_two, indices, blocks, pieces, [a_table])
    inverse = jnp.where(lighter[0], inverse, to_other_core(inverse))
    arrived = [along_groups(value, q + 1) for q, value in enumerate(sends)]
    arrived, keep = lax.optimization_barrier((arrived, keep))
    arrived = [value.astype(F32) for value in arrived]
    own_two = keep + arrived[0] + arrived[1] + arrived[2]
    b_update = jnp.dot(own_two, inverse, precision=HIGHEST)
    return a_update, b_update


def solution(mesh):
    groups, columns = mesh.shape["grp"], mesh.shape["col"]
    side = round((columns // 2) ** 0.5)
    fine = Mesh(mesh.devices.reshape(groups, side, side, 2), ALL)
    row, flat = P(ALL, None), P(ALL)
    return jax.shard_map(
        on_device,
        mesh=fine,
        in_specs=(P(ALL, None, None), flat, flat, flat, flat, row, row),
        out_specs=(row, row),
        check_vma=False,
    )
```

```python
import jax
import jax.numpy as jnp
from jax import lax
from jax.experimental import pallas as pl
from jax.experimental.pallas import tpu as pltpu
from jax.sharding import Mesh
from jax.sharding import PartitionSpec as P

EDGE = 32
GROUP = 8
DEPTH = 4
B_ROWS = 16 * EDGE
C_ROWS = 4 * EDGE
COUNT_ROWS = 16
MODE_COST = pl.CostEstimate(flops=15_000_000_000, bytes_accessed=48_000_000, transcendentals=0)
LAST_PASS_COST = pl.CostEstimate(flops=2_000_000_000, bytes_accessed=6_000_000, transcendentals=0)
INVERSE_COST = pl.CostEstimate(flops=16_000_000_000, bytes_accessed=50_000_000, transcendentals=0)
VMEM_BYTES = 48 << 20
ALL = ("grp", "x", "z", "core")
PLANE = ("x", "z")
CHIPS = ("grp", "x", "z")
RING = ("grp", "core")
F32 = jnp.float32
BF16 = jnp.bfloat16
HIGHEST = lax.Precision.HIGHEST


def invert_four(p):
    inv_det = 1.0 / (p[0][0] * p[1][1] - p[0][1] * p[0][1])
    a00, a01, a11 = p[1][1] * inv_det, -p[0][1] * inv_det, p[0][0] * inv_det
    t00 = a00 * p[0][2] + a01 * p[1][2]
    t01 = a00 * p[0][3] + a01 * p[1][3]
    t10 = a01 * p[0][2] + a11 * p[1][2]
    t11 = a01 * p[0][3] + a11 * p[1][3]
    s00 = p[2][2] - (p[0][2] * t00 + p[1][2] * t10)
    s01 = p[2][3] - (p[0][2] * t01 + p[1][2] * t11)
    s11 = p[3][3] - (p[0][3] * t01 + p[1][3] * t11)
    inv_det = 1.0 / (s00 * s11 - s01 * s01)
    z00, z01, z11 = s11 * inv_det, -s01 * inv_det, s00 * inv_det
    u00, u01 = t00 * z00 + t01 * z01, t00 * z01 + t01 * z11
    u10, u11 = t10 * z00 + t11 * z01, t10 * z01 + t11 * z11
    x00 = a00 + (u00 * t00 + u01 * t01)
    x01 = a01 + (u00 * t10 + u01 * t11)
    x11 = a11 + (u10 * t10 + u11 * t11)
    return [
        [x00, x01, -u00, -u01],
        [x01, x11, -u10, -u11],
        [-u00, -u10, z00, z01],
        [-u01, -u11, z01, z11],
    ]


def invert_block(w):
    n = w.shape[0]
    row = lax.broadcasted_iota(jnp.int32, (n, n), 0)
    col = lax.broadcasted_iota(jnp.int32, (n, n), 1)
    for k in range(0, n, 4):
        cols = [jnp.broadcast_to(w[:, k + q : k + q + 1], (n, n)) for q in range(4)]
        rows = [w[k + q : k + q + 1, :] for q in range(4)]
        pivot = [[cols[b][k + a : k + a + 1, :] for b in range(4)] for a in range(4)]
        inv = invert_four(pivot)
        lane = col[0:1, :]
        fresh = []
        for a in range(4):
            value = (inv[a][0] * rows[0] + inv[a][1] * rows[1]) + (
                inv[a][2] * rows[2] + inv[a][3] * rows[3]
            )
            for b in range(4):
                value = jnp.where(lane == k + b, inv[a][b], value)
            fresh.append(value)
        in_cols = (col >= k) & (col < k + 4)
        in_rows = (row >= k) & (row < k + 4)
        base = jnp.where(in_cols, 0.0, w)
        update = (cols[0] * fresh[0] + cols[1] * fresh[1]) + (
            cols[2] * fresh[2] + cols[3] * fresh[3]
        )
        out = base - update
        for a in range(4):
            out = jnp.where(row == k + a, fresh[a], out)
        w = out
    return w


def tiles_of(matrix):
    across = matrix.shape[1] // 128
    return [
        (r * across + c, slice(r * 8, r * 8 + 8), slice(c * 128, c * 128 + 128))
        for r in range(matrix.shape[0] // 8)
        for c in range(across)
    ]


def invert(out, work):
    n = work.shape[0]
    width = 64
    row = lax.broadcasted_iota(jnp.int32, (n, n), 0)
    col = lax.broadcasted_iota(jnp.int32, (n, n), 1)
    diag = jnp.where(row == col, work[...], 0.0)
    scale_row = lax.rsqrt(jnp.sum(diag, axis=0, keepdims=True))
    scale_col = lax.rsqrt(jnp.sum(diag, axis=1, keepdims=True))
    work[...] = work[...] * scale_row * scale_col
    for b in range(n // width):
        span = slice(b * width, (b + 1) * width)
        block = invert_block(work[span, span])
        rows = jnp.dot(block, work[span, :], precision=HIGHEST, preferred_element_type=F32)
        parts = [jnp.zeros((width, width), F32)] * (n // width)
        parts[b] = block
        padded = jnp.concatenate(parts, axis=1)
        in_block = (col >= b * width) & (col < (b + 1) * width)
        rows = jnp.where(in_block[0:width], padded, rows)
        left = work[:, span]
        left_row = row[:, 0:width]
        left = jnp.where((left_row >= b * width) & (left_row < (b + 1) * width), 0.0, left)
        base = jnp.where(in_block, 0.0, work[...])
        work[...] = base - jnp.dot(left, rows, precision=HIGHEST, preferred_element_type=F32)
        work[span, :] = rows
    out[...] = work[...] * scale_row * scale_col


def takes_turn(meta, ring, other_ring):
    mine, other = jnp.max(ring[...]), jnp.max(other_ring[...])
    return (mine < other) | ((mine == other) & (meta[2] == 0))


def first_inverse_kernel(meta, ring, other_ring, near, far, out, work):
    mine = takes_turn(meta, ring, other_ring)

    @pl.when(jnp.logical_not(mine))
    def _():
        out[...] = jnp.zeros_like(out)

    @pl.when(mine)
    def _():
        for t, rows, cols in tiles_of(work):
            work[rows, cols] = near[t] * far[t]
        invert(out, work)


def second_inverse_kernel(
    meta, ring, other_ring, part_0, part_1, part_2, part_3, near, far, out, work
):
    n = work.shape[0]
    mine = takes_turn(meta, ring, other_ring)

    @pl.when(jnp.logical_not(mine))
    def _():
        out[...] = jnp.zeros_like(out)

    @pl.when(mine)
    def _():
        gram = (part_0[...] + part_1[...]) + (part_2[...] + part_3[...])
        row = lax.broadcasted_iota(jnp.int32, (n, n), 0)
        col = lax.broadcasted_iota(jnp.int32, (n, n), 1)
        diag = jnp.where(row == col, gram, 0.0)
        norm_row = jnp.sqrt(jnp.sum(diag, axis=0, keepdims=True) + 1e-06)
        norm_col = jnp.sqrt(jnp.sum(diag, axis=1, keepdims=True) + 1e-06)
        work[...] = gram / (norm_col * norm_row)
        third_is_near = meta[2] == 1
        for t, rows, cols in tiles_of(work):
            work[rows, cols] = work[rows, cols] * jnp.where(third_is_near, near[t], far[t])
        invert(out, work)


def inverse_of(kernel, name, meta, *arrays):
    n = 256
    return pl.pallas_call(
        kernel,
        out_shape=jax.ShapeDtypeStruct((n, n), F32),
        in_specs=[pl.BlockSpec(memory_space=pltpu.SMEM)]
        + [pl.BlockSpec(memory_space=pltpu.VMEM)] * len(arrays),
        out_specs=pl.BlockSpec(memory_space=pltpu.VMEM),
        scratch_shapes=[pltpu.VMEM((n, n), F32)],
        compiler_params=pltpu.CompilerParams(vmem_limit_bytes=VMEM_BYTES),
        cost_estimate=INVERSE_COST,
        name=name,
    )(meta, *arrays)


def prepare_kernel(meta, b_factor, c_factor, own, gram_keep, gram_send):
    rows = b_factor.shape[0]
    core = meta[2]
    own[0:rows, :] = b_factor[...].astype(BF16)
    own[rows : rows + C_ROWS, :] = c_factor[...].astype(BF16)
    count = meta[0].astype(F32)
    own[rows + C_ROWS :, :] = jnp.full((COUNT_ROWS, own.shape[1]), count, F32).astype(BF16)
    for q, ref in enumerate((b_factor, c_factor)):
        gram = lax.dot_general(
            ref[...],
            ref[...],
            (((0,), (0,)), ((), ())),
            precision=HIGHEST,
            preferred_element_type=F32,
        )

        @pl.when(core == q)
        def _():
            for t, r, c in tiles_of(gram):
                gram_keep[t] = gram[r, c]

        @pl.when(core != q)
        def _():
            for t, r, c in tiles_of(gram):
                gram_send[t] = gram[r, c]


def prepare(meta, b_factor, c_factor):
    rank = b_factor.shape[1]
    rows = b_factor.shape[0] + c_factor.shape[0] + COUNT_ROWS
    tiles = jax.ShapeDtypeStruct((rank * rank // 1024, 8, 128), F32)
    return pl.pallas_call(
        prepare_kernel,
        out_shape=[jax.ShapeDtypeStruct((rows, rank), BF16), tiles, tiles],
        in_specs=[pl.BlockSpec(memory_space=pltpu.SMEM)]
        + [pl.BlockSpec(memory_space=pltpu.VMEM)] * 2,
        compiler_params=pltpu.CompilerParams(vmem_limit_bytes=VMEM_BYTES),
        name="prepare",
    )(meta, b_factor, c_factor)


def order_kernel(meta, i_idx, j_idx, k_idx, order_one, order_two):
    slots = i_idx.shape[0]
    count, grp, core = meta[0], meta[1], meta[2]

    def place(s, front_one, front_two, i, j, k):
        entry = s + 256 * (i + 64 * (j + 64 * k))
        one = ((i >> 1) & 1) ^ core
        two = jnp.where((j >> 4) == grp, 0, 1)
        order_one[jnp.where(one == 1, front_one, slots - 1 - (s - front_one))] = entry
        order_two[jnp.where(two == 1, front_two, slots - 1 - (s - front_two))] = entry
        return front_one + one, front_two + two

    def place_four(q, carry):
        found = [(i_idx[4 * q + u], j_idx[4 * q + u], k_idx[4 * q + u]) for u in range(4)]
        for u in range(4):
            carry = place(4 * q + u, *carry, *found[u])
        return carry

    def place_one(s, carry):
        return place(s, *carry, i_idx[s], j_idx[s], k_idx[s])

    zero = (jnp.int32(0), jnp.int32(0))
    fours = count // 4
    ends = lax.fori_loop(4 * fours, count, place_one, lax.fori_loop(0, fours, place_four, zero))
    for order, front in zip((order_one, order_two), ends):
        order[slots] = front
        order[slots + 1] = count - front
        order[slots + 2] = grp
        order[slots + 3] = core


def order_slots(meta, i_index, j_index, k_index):
    table = jax.ShapeDtypeStruct((i_index.shape[0] + 64,), jnp.int32)
    smem = pl.BlockSpec(memory_space=pltpu.SMEM)
    return pl.pallas_call(
        order_kernel,
        out_shape=[table] * 2,
        in_specs=[smem] * 4,
        out_specs=[smem] * 2,
        name="order_slots",
    )(meta, i_index, j_index, k_index)


def block_rows(ref, start):
    return ref[pl.ds(pl.multiple_of(start, EDGE), EDGE), :]


def copy_all(copies):
    for copy in copies:
        copy.start()
    return copies


def wait_all(copies):
    for copy in copies:
        copy.wait()


def for_each_group(first, order, blocks, buffer, sems, prepare_tables, one_slot):
    slots = blocks.shape[0]
    count = order[slots if first else slots + 1]
    groups = (count + GROUP - 1) // GROUP

    def entry_at(place):
        place = jnp.minimum(place, count - 1)
        return order[place if first else slots - 1 - place]

    def copies(group):
        side = group & (DEPTH - 1)
        return [
            pltpu.make_async_copy(
                blocks.at[entry_at(group * GROUP + u) & 255], buffer.at[side, u], sems.at[side, u]
            )
            for u in range(GROUP)
        ]

    for ahead in range(DEPTH - 1):

        @pl.when(ahead < groups)
        def _():
            copy_all(copies(ahead))

    prepare_tables()

    def one_group(group, carry):
        @pl.when(group + DEPTH - 1 < groups)
        def _():
            copy_all(copies(group + DEPTH - 1))

        wait_all(copies(group))
        for u in range(GROUP):
            place = group * GROUP + u
            entry = entry_at(place)
            i, j, k = (entry >> 8) & 63, (entry >> 14) & 63, (entry >> 20) & 15
            one_slot(buffer[group & (DEPTH - 1), u], u, i, j, k, place < count)
        return carry

    lax.fori_loop(0, groups, one_group, 0)


def mode_one_kernel(
    first, order, blocks, own_0, own_1, own_2, own_3, out, *rest
):
    ring = rest[0] if first else None
    buffer, table, acc, sems, table_sems = rest[-5:]
    grp = order[blocks.shape[0] + 2]
    own = own_0.shape[0]
    half = out.shape[0]

    def prepare_tables():
        pieces = copy_all(
            [
                pltpu.make_async_copy(ref, table.at[pl.ds(q * own, own)], table_sems.at[q])
                for q, ref in enumerate((own_0, own_1, own_2, own_3))
            ]
        )
        acc[...] = jnp.zeros_like(acc)
        wait_all(pieces)

    def one_slot(block, u, i, j, k, live):
        b_rows = block_rows(table, ((grp - (j >> 4)) & 3) * own + (j & 15) * EDGE)
        c_rows = block_rows(table, ((grp - (k >> 2)) & 3) * own + B_ROWS + (k & 3) * EDGE)
        product = (b_rows[:, None, :] * c_rows[None, :, :]).reshape(EDGE * EDGE, -1)
        result = jnp.dot(block, product, preferred_element_type=F32)
        target = jnp.where(live, (i >> 2) * (2 * EDGE) + (i & 1) * EDGE, half)
        acc[pl.ds(pl.multiple_of(target, EDGE), EDGE), :] += result

    for_each_group(first, order, blocks, buffer, sems, prepare_tables, one_slot)
    out[...] = acc[0:half, :]
    if first:
        counts = [
            table[(q + 1) * own - COUNT_ROWS : (q + 1) * own, 0:128].astype(F32) for q in range(4)
        ]
        most = jnp.maximum(jnp.maximum(counts[0], counts[1]), jnp.maximum(counts[2], counts[3]))
        ring[...] = most[0:8, :]


def turn_block(block, turned, u):
    lane = lax.broadcasted_iota(jnp.int32, (8, 128), 1)
    low_half = lane < 64
    even_group = (lane // 32) % 2 == 0
    wide = block.astype(F32)
    for jh in range(8):
        t = [wide[il * 8 : il * 8 + 8, jh * 128 : jh * 128 + 128] for il in range(4)]
        m = [None] * 4
        for il in range(2):
            m[il] = jnp.where(low_half, t[il], pltpu.roll(t[il + 2], 64, 1))
            m[il + 2] = jnp.where(low_half, pltpu.roll(t[il], 64, 1), t[il + 2])
        for q in (0, 2):
            j = jh * 4 + q
            turned[u, j * 8 : j * 8 + 8, :] = jnp.where(
                even_group, m[q], pltpu.roll(m[q + 1], 32, 1)
            )
            turned[u, j * 8 + 8 : j * 8 + 16, :] = jnp.where(
                even_group, pltpu.roll(m[q], 96, 1), m[q + 1]
            )
    return jnp.concatenate(
        [turned[u, pl.ds(ih, EDGE, stride=8), :].astype(BF16) for ih in range(8)], axis=1
    )


def mode_two_slots(first, order, blocks, owns, a_table, scratch, part):
    buffer, turned, table, acc, sems, table_sems = scratch
    grp, core = order[blocks.shape[0] + 2], order[blocks.shape[0] + 3]
    half = a_table.shape[0] // 2

    def prepare_tables():
        pieces = copy_all(
            [
                pltpu.make_async_copy(
                    ref.at[pl.ds(B_ROWS, C_ROWS)],
                    table.at[pl.ds(q * C_ROWS, C_ROWS)],
                    table_sems.at[q],
                )
                for q, ref in enumerate(owns)
            ]
        )
        acc[...] = jnp.zeros_like(acc)
        wait_all(pieces)

    def one_slot(block, u, i, j, k, live):
        a_rows = block_rows(
            a_table,
            (((i >> 1) & 1) ^ core) * half + (i >> 2) * (2 * EDGE) + (i & 1) * EDGE,
        )
        c_rows = block_rows(table, ((grp - (k >> 2)) & 3) * C_ROWS + (k & 3) * EDGE)
        left = turn_block(block, turned, u)
        product = jnp.concatenate(
            [
                a_rows[il * 8 + ih : il * 8 + ih + 1, :] * c_rows
                for ih in range(8)
                for il in range(4)
            ],
            axis=0,
        )
        result = jnp.dot(left, product, preferred_element_type=F32)
        target = (j & 15) * EDGE
        if first:
            target += (((j >> 4) - grp - 1) & 3) * part
        target = jnp.where(live, target, acc.shape[0] - EDGE)
        acc[pl.ds(pl.multiple_of(target, EDGE), EDGE), :] += result

    for_each_group(first, order, blocks, buffer, sems, prepare_tables, one_slot)


def mode_two_others_kernel(
    order,
    blocks,
    own_0,
    own_1,
    own_2,
    own_3,
    a_near,
    a_far,
    squares,
    send_1,
    send_2,
    send_3,
    a_table,
    *scratch,
):
    half = a_near.shape[0]
    part = send_1.shape[0]
    col_norm = jnp.sqrt(squares[...] + 1e-06)
    a_table[0:half, :] = (a_near[...] / col_norm).astype(BF16)
    a_table[half : 2 * half, :] = (a_far[...] / col_norm).astype(BF16)
    mode_two_slots(True, order, blocks, (own_0, own_1, own_2, own_3), a_table, scratch, part)
    acc = scratch[3]
    for q, ref in enumerate((send_1, send_2, send_3)):
        ref[...] = acc[q * part : (q + 1) * part, :].astype(BF16)


def mode_two_own_kernel(order, blocks, own_0, own_1, own_2, own_3, a_table, keep, *scratch):
    part = keep.shape[0]
    mode_two_slots(False, order, blocks, (own_0, own_1, own_2, own_3), a_table, scratch, part)
    keep[...] = scratch[3][0:part, :]


def mode_call(kernel, name, order, in_place, resident, out_shape, scratch):
    smem, anywhere, vmem = (
        pl.BlockSpec(memory_space=pltpu.SMEM),
        pl.BlockSpec(memory_space=pl.ANY),
        pl.BlockSpec(memory_space=pltpu.VMEM),
    )
    blocks = in_place[0]
    buffer = pltpu.VMEM((DEPTH, GROUP) + blocks.shape[1:], blocks.dtype)
    return pl.pallas_call(
        kernel,
        out_shape=out_shape,
        in_specs=[smem] + [anywhere] * len(in_place) + [vmem] * len(resident),
        out_specs=[vmem] * len(out_shape),
        scratch_shapes=[buffer]
        + scratch
        + [pltpu.SemaphoreType.DMA((DEPTH, GROUP)), pltpu.SemaphoreType.DMA((4,))],
        compiler_params=pltpu.CompilerParams(vmem_limit_bytes=VMEM_BYTES),
        cost_estimate=LAST_PASS_COST if name == "mode_two_own_group" else MODE_COST,
        name=name,
    )(order, *in_place, *resident)


def mode_one(first, order, blocks, pieces):
    own, rank = pieces[0].shape
    half = 32 * EDGE

    def kernel(*refs):
        mode_one_kernel(first, *refs)

    return mode_call(
        kernel,
        "mode_one_other_core" if first else "mode_one_own_core",
        order,
        [blocks] + pieces,
        [],
        [jax.ShapeDtypeStruct((half, rank), F32)]
        + ([jax.ShapeDtypeStruct((8, 128), F32)] if first else []),
        [pltpu.VMEM((4 * own, rank), BF16), pltpu.VMEM((half + EDGE, rank), F32)],
    )


def mode_two(first, order, blocks, pieces, resident):
    rank = pieces[0].shape[1]
    part = 16 * EDGE
    sent = jax.ShapeDtypeStruct((part, rank), BF16)
    if first:
        out_shape = [sent] * 3 + [jax.ShapeDtypeStruct((64 * EDGE, rank), BF16)]
    else:
        out_shape = [jax.ShapeDtypeStruct((part, rank), F32)]
    return mode_call(
        mode_two_others_kernel if first else mode_two_own_kernel,
        "mode_two_other_groups" if first else "mode_two_own_group",
        order,
        [blocks] + pieces,
        resident,
        out_shape,
        [
            pltpu.VMEM((GROUP, 8 * EDGE, 128), F32),
            pltpu.VMEM((4 * C_ROWS, rank), BF16),
            pltpu.VMEM(((3 if first else 1) * part + EDGE, rank), F32),
        ],
    )


def to_other_core(value):
    return lax.ppermute(value, "core", [(0, 1), (1, 0)])


def along_groups(value, shift):
    size = lax.axis_size("grp")
    return lax.ppermute(value, "grp", [(p, (p + shift) % size) for p in range(size)])


def exchange(value, axes):
    return lax.all_to_all(value, axes, 0, 0)


def on_device(blocks, i_index, j_index, k_index, block_count, b_factor, c_factor):
    rank = b_factor.shape[1]
    grp, core = lax.axis_index("grp"), lax.axis_index("core")
    plane = lax.axis_size(PLANE)
    chips = lax.axis_size(CHIPS)
    ring_size = lax.axis_size(RING)
    meta = jnp.stack([block_count[0], grp, core])

    own, gram_keep, gram_send = prepare(meta, b_factor, c_factor)
    order_one, order_two = order_slots(meta, i_index, j_index, k_index)
    gram_pair = gram_keep + to_other_core(gram_send)
    pieces = [own] + [along_groups(own, q) for q in (1, 2, 3)]
    gram_parts = exchange(gram_pair.reshape(chips, -1, 8, 128), CHIPS)
    send, ring = mode_one(True, order_one, blocks, pieces)
    piece = jnp.sum(gram_parts, axis=0)
    piece, send = lax.optimization_barrier((piece, send))
    spread = jnp.broadcast_to(piece[None], (chips,) + piece.shape)
    spread, pieces = lax.optimization_barrier((spread, pieces))
    gram_near = exchange(spread, CHIPS)
    [keep] = mode_one(False, order_one, blocks, pieces)
    gram_near, keep = lax.optimization_barrier((gram_near, keep))
    gram_near = gram_near.reshape(-1, 8, 128)
    gram_far = to_other_core(gram_near)
    rings = (ring, to_other_core(ring))

    pair_sum = (keep + to_other_core(send)).astype(BF16)
    arrived = exchange(pair_sum.reshape(plane, -1, rank), PLANE)
    sum_own = jnp.sum(arrived.astype(F32), axis=0)
    sum_near = exchange(jnp.broadcast_to(sum_own[None], (plane,) + sum_own.shape), PLANE)
    sum_near = sum_near.reshape(-1, rank)

    inverse = inverse_of(first_inverse_kernel, "first_inverse", meta, *rings, gram_near, gram_far)
    mine, other = rings[0][0, 0], rings[1][0, 0]
    lighter = (mine < other) | ((mine == other) & (core == 0))
    inverse = jnp.where(lighter, inverse, to_other_core(inverse))

    sum_far = to_other_core(sum_near)
    a_near = jnp.dot(sum_near, inverse, precision=HIGHEST)
    squares = jnp.sum(a_near * a_near, axis=0, keepdims=True)
    squares = exchange(jnp.broadcast_to(squares[None], (ring_size,) + squares.shape), RING)
    squares = jnp.sum(squares, axis=0)
    a_far = jnp.dot(sum_far, inverse, precision=HIGHEST)
    gram_core = jnp.dot(a_near.T, a_near, precision=HIGHEST)
    gram_plane = gram_core + to_other_core(gram_core)
    gram_parts = [gram_plane] + [along_groups(gram_plane, q) for q in (1, 2, 3)]

    *sends, a_table = mode_two(True, order_two, blocks, pieces, [a_near, a_far, squares])
    gram_parts, sends = lax.optimization_barrier((gram_parts, sends))
    second = inverse_of(
        second_inverse_kernel, "second_inverse", meta, *rings, *gram_parts, gram_near, gram_far
    )
    second, a_table = lax.optimization_barrier((second, a_table))
    [keep] = mode_two(False, order_two, blocks, pieces, [a_table])
    a_update = jnp.dot(sum_own, inverse, precision=HIGHEST)
    arrived = [along_groups(value, q + 1) for q, value in enumerate(sends)]
    arrived, keep, second = lax.optimization_barrier((arrived, keep, second))
    second = jnp.where(lighter, second, to_other_core(second))
    arrived = [value.astype(F32) for value in arrived]
    own_two = keep + arrived[0] + arrived[1] + arrived[2]
    b_update = jnp.dot(own_two, second, precision=HIGHEST)
    return a_update, b_update


def solution(mesh):
    groups, columns = mesh.shape["grp"], mesh.shape["col"]
    side = round((columns // 2) ** 0.5)
    fine = Mesh(mesh.devices.reshape(groups, side, side, 2), ALL)
    row, flat = P(ALL, None), P(ALL)
    return jax.shard_map(
        on_device,
        mesh=fine,
        in_specs=(P(ALL, None, None), flat, flat, flat, flat, row, row),
        out_specs=(row, row),
        check_vma=False,
    )
```

```python
import jax
import jax.numpy as jnp
from jax import lax
from jax.experimental import pallas as pl
from jax.experimental.pallas import tpu as pltpu
from jax.sharding import Mesh
from jax.sharding import PartitionSpec as P

EDGE = 32
GROUP = 8
DEPTH = 4
B_ROWS = 16 * EDGE
C_ROWS = 4 * EDGE
COUNT_ROWS = 16
MODE_COST = pl.CostEstimate(flops=15_000_000_000, bytes_accessed=48_000_000, transcendentals=0)
LAST_PASS_COST = pl.CostEstimate(flops=2_000_000_000, bytes_accessed=6_000_000, transcendentals=0)
INVERSE_COST = pl.CostEstimate(flops=16_000_000_000, bytes_accessed=50_000_000, transcendentals=0)
VMEM_BYTES = 8 << 20
MODE_VMEM_BYTES = 48 << 20
ALL = ("grp", "x", "z", "core")
PLANE = ("x", "z")
CHIPS = ("grp", "x", "z")
F32 = jnp.float32
BF16 = jnp.bfloat16
HIGHEST = lax.Precision.HIGHEST


def invert_four(p):
    inv_det = 1.0 / (p[0][0] * p[1][1] - p[0][1] * p[0][1])
    a00, a01, a11 = p[1][1] * inv_det, -p[0][1] * inv_det, p[0][0] * inv_det
    t00 = a00 * p[0][2] + a01 * p[1][2]
    t01 = a00 * p[0][3] + a01 * p[1][3]
    t10 = a01 * p[0][2] + a11 * p[1][2]
    t11 = a01 * p[0][3] + a11 * p[1][3]
    s00 = p[2][2] - (p[0][2] * t00 + p[1][2] * t10)
    s01 = p[2][3] - (p[0][2] * t01 + p[1][2] * t11)
    s11 = p[3][3] - (p[0][3] * t01 + p[1][3] * t11)
    inv_det = 1.0 / (s00 * s11 - s01 * s01)
    z00, z01, z11 = s11 * inv_det, -s01 * inv_det, s00 * inv_det
    u00, u01 = t00 * z00 + t01 * z01, t00 * z01 + t01 * z11
    u10, u11 = t10 * z00 + t11 * z01, t10 * z01 + t11 * z11
    x00 = a00 + (u00 * t00 + u01 * t01)
    x01 = a01 + (u00 * t10 + u01 * t11)
    x11 = a11 + (u10 * t10 + u11 * t11)
    return [
        [x00, x01, -u00, -u01],
        [x01, x11, -u10, -u11],
        [-u00, -u10, z00, z01],
        [-u01, -u11, z01, z11],
    ]


def invert_block(w):
    n = w.shape[0]
    row = lax.broadcasted_iota(jnp.int32, (n, n), 0)
    col = lax.broadcasted_iota(jnp.int32, (n, n), 1)
    for k in range(0, n, 4):
        cols = [jnp.broadcast_to(w[:, k + q : k + q + 1], (n, n)) for q in range(4)]
        rows = [w[k + q : k + q + 1, :] for q in range(4)]
        pivot = [[cols[b][k + a : k + a + 1, :] for b in range(4)] for a in range(4)]
        inv = invert_four(pivot)
        lane = col[0:1, :]
        fresh = []
        for a in range(4):
            value = (inv[a][0] * rows[0] + inv[a][1] * rows[1]) + (
                inv[a][2] * rows[2] + inv[a][3] * rows[3]
            )
            for b in range(4):
                value = jnp.where(lane == k + b, inv[a][b], value)
            fresh.append(value)
        in_cols = (col >= k) & (col < k + 4)
        in_rows = (row >= k) & (row < k + 4)
        base = jnp.where(in_cols, 0.0, w)
        update = (cols[0] * fresh[0] + cols[1] * fresh[1]) + (
            cols[2] * fresh[2] + cols[3] * fresh[3]
        )
        out = base - update
        for a in range(4):
            out = jnp.where(row == k + a, fresh[a], out)
        w = out
    return w


def tiles_of(matrix):
    across = matrix.shape[1] // 128
    return [
        (r * across + c, slice(r * 8, r * 8 + 8), slice(c * 128, c * 128 + 128))
        for r in range(matrix.shape[0] // 8)
        for c in range(across)
    ]


def invert(out, work):
    n = work.shape[0]
    width = 64
    row = lax.broadcasted_iota(jnp.int32, (n, n), 0)
    col = lax.broadcasted_iota(jnp.int32, (n, n), 1)
    diag = jnp.where(row == col, work[...], 0.0)
    scale_row = lax.rsqrt(jnp.sum(diag, axis=0, keepdims=True))
    scale_col = lax.rsqrt(jnp.sum(diag, axis=1, keepdims=True))
    work[...] = work[...] * scale_row * scale_col
    for b in range(n // width):
        span = slice(b * width, (b + 1) * width)
        block = invert_block(work[span, span])
        rows = jnp.dot(block, work[span, :], precision=HIGHEST, preferred_element_type=F32)
        parts = [jnp.zeros((width, width), F32)] * (n // width)
        parts[b] = block
        padded = jnp.concatenate(parts, axis=1)
        in_block = (col >= b * width) & (col < (b + 1) * width)
        rows = jnp.where(in_block[0:width], padded, rows)
        left = work[:, span]
        left_row = row[:, 0:width]
        left = jnp.where((left_row >= b * width) & (left_row < (b + 1) * width), 0.0, left)
        base = jnp.where(in_block, 0.0, work[...])
        work[...] = base - jnp.dot(left, rows, precision=HIGHEST, preferred_element_type=F32)
        work[span, :] = rows
    out[...] = work[...] * scale_row * scale_col


def takes_turn(meta, ring, other_ring):
    mine, other = jnp.max(ring[...]), jnp.max(other_ring[...])
    return (mine < other) | ((mine == other) & (meta[2] == 0))


def first_inverse_kernel(meta, ring, other_ring, near, far, out, work):
    mine = takes_turn(meta, ring, other_ring)

    @pl.when(jnp.logical_not(mine))
    def _():
        out[...] = jnp.zeros_like(out)

    @pl.when(mine)
    def _():
        for t, rows, cols in tiles_of(work):
            work[rows, cols] = near[t] * far[t]
        invert(out, work)


def second_inverse_kernel(
    meta, ring, other_ring, part_0, part_1, part_2, part_3, near, far, out, work
):
    n = work.shape[0]
    mine = takes_turn(meta, ring, other_ring)

    @pl.when(jnp.logical_not(mine))
    def _():
        out[...] = jnp.zeros_like(out)

    @pl.when(mine)
    def _():
        gram = (part_0[...] + part_1[...]) + (part_2[...] + part_3[...])
        row = lax.broadcasted_iota(jnp.int32, (n, n), 0)
        col = lax.broadcasted_iota(jnp.int32, (n, n), 1)
        diag = jnp.where(row == col, gram, 0.0)
        norm_row = jnp.sqrt(jnp.sum(diag, axis=0, keepdims=True) + 1e-06)
        norm_col = jnp.sqrt(jnp.sum(diag, axis=1, keepdims=True) + 1e-06)
        work[...] = gram / (norm_col * norm_row)
        third_is_near = meta[2] == 1
        for t, rows, cols in tiles_of(work):
            work[rows, cols] = work[rows, cols] * jnp.where(third_is_near, near[t], far[t])
        invert(out, work)


def inverse_of(kernel, name, meta, *arrays):
    n = 256
    return pl.pallas_call(
        kernel,
        out_shape=jax.ShapeDtypeStruct((n, n), F32),
        in_specs=[pl.BlockSpec(memory_space=pltpu.SMEM)]
        + [pl.BlockSpec(memory_space=pltpu.VMEM)] * len(arrays),
        out_specs=pl.BlockSpec(memory_space=pltpu.VMEM),
        scratch_shapes=[pltpu.VMEM((n, n), F32)],
        compiler_params=pltpu.CompilerParams(vmem_limit_bytes=VMEM_BYTES),
        cost_estimate=INVERSE_COST,
        name=name,
    )(meta, *arrays)


def prepare_kernel(meta, b_hbm, c_hbm, own, gram_keep, gram_send, b_factor, c_factor, sems):
    rows = b_factor.shape[0]
    core = meta[2]
    wait_all(
        copy_all(
            [
                pltpu.make_async_copy(b_hbm, b_factor, sems.at[0]),
                pltpu.make_async_copy(c_hbm, c_factor, sems.at[1]),
            ]
        )
    )
    own[0:rows, :] = b_factor[...].astype(BF16)
    own[rows : rows + C_ROWS, :] = c_factor[...].astype(BF16)
    count = meta[0].astype(F32)
    own[rows + C_ROWS :, :] = jnp.full((COUNT_ROWS, own.shape[1]), count, F32).astype(BF16)
    for q, ref in enumerate((b_factor, c_factor)):
        gram = lax.dot_general(
            ref[...],
            ref[...],
            (((0,), (0,)), ((), ())),
            precision=HIGHEST,
            preferred_element_type=F32,
        )

        @pl.when(core == q)
        def _():
            for t, r, c in tiles_of(gram):
                gram_keep[t] = gram[r, c]

        @pl.when(core != q)
        def _():
            for t, r, c in tiles_of(gram):
                gram_send[t] = gram[r, c]


def prepare(meta, b_factor, c_factor):
    rank = b_factor.shape[1]
    rows = b_factor.shape[0] + c_factor.shape[0] + COUNT_ROWS
    tiles = jax.ShapeDtypeStruct((rank * rank // 1024, 8, 128), F32)
    return pl.pallas_call(
        prepare_kernel,
        out_shape=[jax.ShapeDtypeStruct((rows, rank), BF16), tiles, tiles],
        in_specs=[pl.BlockSpec(memory_space=pltpu.SMEM)]
        + [pl.BlockSpec(memory_space=pl.ANY)] * 2,
        scratch_shapes=[
            pltpu.VMEM(b_factor.shape, F32),
            pltpu.VMEM(c_factor.shape, F32),
            pltpu.SemaphoreType.DMA((2,)),
        ],
        compiler_params=pltpu.CompilerParams(vmem_limit_bytes=VMEM_BYTES),
        name="prepare",
    )(meta, b_factor, c_factor)


def order_kernel(meta, i_idx, j_idx, k_idx, order_one, order_two):
    slots = i_idx.shape[0]
    count, grp, core = meta[0], meta[1], meta[2]

    def place(s, front_one, front_two, i, j, k):
        entry = s + 256 * (i + 64 * (j + 64 * k))
        one = ((i >> 1) & 1) ^ core
        two = jnp.where((j >> 4) == grp, 0, 1)
        order_one[jnp.where(one == 1, front_one, slots - 1 - (s - front_one))] = entry
        order_two[jnp.where(two == 1, front_two, slots - 1 - (s - front_two))] = entry
        return front_one + one, front_two + two

    def place_four(q, carry):
        found = [(i_idx[4 * q + u], j_idx[4 * q + u], k_idx[4 * q + u]) for u in range(4)]
        for u in range(4):
            carry = place(4 * q + u, *carry, *found[u])
        return carry

    def place_one(s, carry):
        return place(s, *carry, i_idx[s], j_idx[s], k_idx[s])

    zero = (jnp.int32(0), jnp.int32(0))
    fours = count // 4
    ends = lax.fori_loop(4 * fours, count, place_one, lax.fori_loop(0, fours, place_four, zero))
    for order, front in zip((order_one, order_two), ends):
        order[slots] = front
        order[slots + 1] = count - front
        order[slots + 2] = grp
        order[slots + 3] = core


def order_slots(meta, i_index, j_index, k_index):
    table = jax.ShapeDtypeStruct((i_index.shape[0] + 64,), jnp.int32)
    smem = pl.BlockSpec(memory_space=pltpu.SMEM)
    return pl.pallas_call(
        order_kernel,
        out_shape=[table] * 2,
        in_specs=[smem] * 4,
        out_specs=[smem] * 2,
        name="order_slots",
    )(meta, i_index, j_index, k_index)


def block_rows(ref, start):
    return ref[pl.ds(pl.multiple_of(start, EDGE), EDGE), :]


def copy_all(copies):
    for copy in copies:
        copy.start()
    return copies


def wait_all(copies):
    for copy in copies:
        copy.wait()


def for_each_group(first, order, blocks, buffer, sems, prepare_tables, one_slot):
    slots = blocks.shape[0]
    count = order[slots if first else slots + 1]
    groups = (count + GROUP - 1) // GROUP

    def entry_at(place):
        place = jnp.minimum(place, count - 1)
        return order[place if first else slots - 1 - place]

    def copies(group):
        side = group & (DEPTH - 1)
        return [
            pltpu.make_async_copy(
                blocks.at[entry_at(group * GROUP + u) & 255], buffer.at[side, u], sems.at[side, u]
            )
            for u in range(GROUP)
        ]

    for ahead in range(DEPTH - 1):

        @pl.when(ahead < groups)
        def _():
            copy_all(copies(ahead))

    prepare_tables()

    def one_group(group, carry):
        @pl.when(group + DEPTH - 1 < groups)
        def _():
            copy_all(copies(group + DEPTH - 1))

        wait_all(copies(group))
        for u in range(GROUP):
            place = group * GROUP + u
            entry = entry_at(place)
            i, j, k = (entry >> 8) & 63, (entry >> 14) & 63, (entry >> 20) & 15
            one_slot(buffer[group & (DEPTH - 1), u], u, i, j, k, place < count)
        return carry

    lax.fori_loop(0, groups, one_group, 0)


def mode_one_kernel(
    first, order, blocks, own_0, own_1, own_2, own_3, out, *rest
):
    ring = rest[0] if first else None
    buffer, table, acc, sems, table_sems = rest[-5:]
    grp = order[blocks.shape[0] + 2]
    own = own_0.shape[0]
    half = out.shape[0]

    def prepare_tables():
        pieces = copy_all(
            [
                pltpu.make_async_copy(ref, table.at[pl.ds(q * own, own)], table_sems.at[q])
                for q, ref in enumerate((own_0, own_1, own_2, own_3))
            ]
        )
        acc[...] = jnp.zeros_like(acc)
        wait_all(pieces)

    def one_slot(block, u, i, j, k, live):
        b_rows = block_rows(table, ((grp - (j >> 4)) & 3) * own + (j & 15) * EDGE)
        c_rows = block_rows(table, ((grp - (k >> 2)) & 3) * own + B_ROWS + (k & 3) * EDGE)
        product = (b_rows[:, None, :] * c_rows[None, :, :]).reshape(EDGE * EDGE, -1)
        result = jnp.dot(block, product, preferred_element_type=F32)
        target = jnp.where(live, (i >> 2) * (2 * EDGE) + (i & 1) * EDGE, half)
        acc[pl.ds(pl.multiple_of(target, EDGE), EDGE), :] += result

    for_each_group(first, order, blocks, buffer, sems, prepare_tables, one_slot)
    out[...] = acc[0:half, :]
    if first:
        counts = [
            table[(q + 1) * own - COUNT_ROWS : (q + 1) * own, 0:128].astype(F32) for q in range(4)
        ]
        most = jnp.maximum(jnp.maximum(counts[0], counts[1]), jnp.maximum(counts[2], counts[3]))
        ring[...] = most[0:8, :]


def turn_block(block, turned, u):
    lane = lax.broadcasted_iota(jnp.int32, (8, 128), 1)
    low_half = lane < 64
    even_group = (lane // 32) % 2 == 0
    wide = block.astype(F32)
    for jh in range(8):
        t = [wide[il * 8 : il * 8 + 8, jh * 128 : jh * 128 + 128] for il in range(4)]
        m = [None] * 4
        for il in range(2):
            m[il] = jnp.where(low_half, t[il], pltpu.roll(t[il + 2], 64, 1))
            m[il + 2] = jnp.where(low_half, pltpu.roll(t[il], 64, 1), t[il + 2])
        for q in (0, 2):
            j = jh * 4 + q
            turned[u, j * 8 : j * 8 + 8, :] = jnp.where(
                even_group, m[q], pltpu.roll(m[q + 1], 32, 1)
            )
            turned[u, j * 8 + 8 : j * 8 + 16, :] = jnp.where(
                even_group, pltpu.roll(m[q], 96, 1), m[q + 1]
            )
    return jnp.concatenate(
        [turned[u, pl.ds(ih, EDGE, stride=8), :].astype(BF16) for ih in range(8)], axis=1
    )


def mode_two_slots(first, order, blocks, owns, a_table, scratch, part):
    buffer, turned, table, acc, sems, table_sems = scratch
    grp, core = order[blocks.shape[0] + 2], order[blocks.shape[0] + 3]
    half = a_table.shape[0] // 2

    def prepare_tables():
        pieces = copy_all(
            [
                pltpu.make_async_copy(
                    ref.at[pl.ds(B_ROWS, C_ROWS)],
                    table.at[pl.ds(q * C_ROWS, C_ROWS)],
                    table_sems.at[q],
                )
                for q, ref in enumerate(owns)
            ]
        )
        acc[...] = jnp.zeros_like(acc)
        wait_all(pieces)

    def one_slot(block, u, i, j, k, live):
        a_rows = block_rows(
            a_table,
            (((i >> 1) & 1) ^ core) * half + (i >> 2) * (2 * EDGE) + (i & 1) * EDGE,
        )
        c_rows = block_rows(table, ((grp - (k >> 2)) & 3) * C_ROWS + (k & 3) * EDGE)
        left = turn_block(block, turned, u)
        product = jnp.concatenate(
            [
                a_rows[il * 8 + ih : il * 8 + ih + 1, :] * c_rows
                for ih in range(8)
                for il in range(4)
            ],
            axis=0,
        )
        result = jnp.dot(left, product, preferred_element_type=F32)
        target = (j & 15) * EDGE
        if first:
            target += (((j >> 4) - grp - 1) & 3) * part
        target = jnp.where(live, target, acc.shape[0] - EDGE)
        acc[pl.ds(pl.multiple_of(target, EDGE), EDGE), :] += result

    for_each_group(first, order, blocks, buffer, sems, prepare_tables, one_slot)


def mode_two_others_kernel(
    order,
    blocks,
    own_0,
    own_1,
    own_2,
    own_3,
    a_near,
    a_far,
    squares,
    send_1,
    send_2,
    send_3,
    a_table,
    *scratch,
):
    half = a_near.shape[0]
    part = send_1.shape[0]
    inv_norm = 1.0 / jnp.sqrt(squares[...] + 1e-06)
    a_table[0:half, :] = (a_near[...] * inv_norm).astype(BF16)
    a_table[half : 2 * half, :] = (a_far[...] * inv_norm).astype(BF16)
    mode_two_slots(True, order, blocks, (own_0, own_1, own_2, own_3), a_table, scratch, part)
    acc = scratch[3]
    for q, ref in enumerate((send_1, send_2, send_3)):
        ref[...] = acc[q * part : (q + 1) * part, :].astype(BF16)


def mode_two_own_kernel(order, blocks, own_0, own_1, own_2, own_3, a_table, keep, *scratch):
    part = keep.shape[0]
    mode_two_slots(False, order, blocks, (own_0, own_1, own_2, own_3), a_table, scratch, part)
    keep[...] = scratch[3][0:part, :]


def mode_call(kernel, name, order, in_place, resident, out_shape, scratch):
    smem, anywhere, vmem = (
        pl.BlockSpec(memory_space=pltpu.SMEM),
        pl.BlockSpec(memory_space=pl.ANY),
        pl.BlockSpec(memory_space=pltpu.VMEM),
    )
    blocks = in_place[0]
    buffer = pltpu.VMEM((DEPTH, GROUP) + blocks.shape[1:], blocks.dtype)
    return pl.pallas_call(
        kernel,
        out_shape=out_shape,
        in_specs=[smem] + [anywhere] * len(in_place) + [vmem] * len(resident),
        out_specs=[vmem] * len(out_shape),
        scratch_shapes=[buffer]
        + scratch
        + [pltpu.SemaphoreType.DMA((DEPTH, GROUP)), pltpu.SemaphoreType.DMA((4,))],
        compiler_params=pltpu.CompilerParams(vmem_limit_bytes=MODE_VMEM_BYTES),
        cost_estimate=LAST_PASS_COST if name == "mode_two_own_group" else MODE_COST,
        name=name,
    )(order, *in_place, *resident)


def mode_one(first, order, blocks, pieces):
    own, rank = pieces[0].shape
    half = 32 * EDGE

    def kernel(*refs):
        mode_one_kernel(first, *refs)

    return mode_call(
        kernel,
        "mode_one_other_core" if first else "mode_one_own_core",
        order,
        [blocks] + pieces,
        [],
        [jax.ShapeDtypeStruct((half, rank), F32)]
        + ([jax.ShapeDtypeStruct((8, 128), F32)] if first else []),
        [pltpu.VMEM((4 * own, rank), BF16), pltpu.VMEM((half + EDGE, rank), F32)],
    )


def mode_two(first, order, blocks, pieces, resident):
    rank = pieces[0].shape[1]
    part = 16 * EDGE
    sent = jax.ShapeDtypeStruct((part, rank), BF16)
    if first:
        out_shape = [sent] * 3 + [jax.ShapeDtypeStruct((64 * EDGE, rank), BF16)]
    else:
        out_shape = [jax.ShapeDtypeStruct((part, rank), F32)]
    return mode_call(
        mode_two_others_kernel if first else mode_two_own_kernel,
        "mode_two_other_groups" if first else "mode_two_own_group",
        order,
        [blocks] + pieces,
        resident,
        out_shape,
        [
            pltpu.VMEM((GROUP, 8 * EDGE, 128), F32),
            pltpu.VMEM((4 * C_ROWS, rank), BF16),
            pltpu.VMEM(((3 if first else 1) * part + EDGE, rank), F32),
        ],
    )


def to_other_core(value):
    return lax.ppermute(value, "core", [(0, 1), (1, 0)])


def along_groups(value, shift):
    size = lax.axis_size("grp")
    return lax.ppermute(value, "grp", [(p, (p + shift) % size) for p in range(size)])


def exchange(value, axes):
    return lax.all_to_all(value, axes, 0, 0)


def on_device(blocks, i_index, j_index, k_index, block_count, b_factor, c_factor):
    rank = b_factor.shape[1]
    grp, core = lax.axis_index("grp"), lax.axis_index("core")
    plane = lax.axis_size(PLANE)
    chips = lax.axis_size(CHIPS)
    meta = jnp.stack([block_count[0], grp, core])

    own, gram_keep, gram_send = prepare(meta, b_factor, c_factor)
    gram_pair = gram_keep + to_other_core(gram_send)
    gram_pair, late_meta = lax.optimization_barrier((gram_pair, meta))
    order_one, order_two = order_slots(late_meta, i_index, j_index, k_index)
    pieces = [own] + [along_groups(own, q) for q in (1, 2, 3)]
    gram_parts = exchange(gram_pair.reshape(chips, -1, 8, 128), CHIPS)
    send, ring = mode_one(True, order_one, blocks, pieces)
    piece = jnp.sum(gram_parts, axis=0)
    piece, send = lax.optimization_barrier((piece, send))
    spread = jnp.broadcast_to(piece[None], (chips,) + piece.shape)
    spread, pieces = lax.optimization_barrier((spread, pieces))
    gram_near = exchange(spread, CHIPS)
    [keep] = mode_one(False, order_one, blocks, pieces)
    gram_near, keep = lax.optimization_barrier((gram_near, keep))
    gram_near = gram_near.reshape(-1, 8, 128)
    gram_far = to_other_core(gram_near)
    rings = (ring, to_other_core(ring))

    pair_sum = (keep + to_other_core(send)).astype(BF16)
    arrived = exchange(pair_sum.reshape(plane, -1, rank), PLANE)
    sum_own = jnp.sum(arrived.astype(F32), axis=0)
    sum_near = exchange(jnp.broadcast_to(sum_own[None], (plane,) + sum_own.shape), PLANE)
    sum_near = sum_near.reshape(-1, rank)

    inverse = inverse_of(first_inverse_kernel, "first_inverse", meta, *rings, gram_near, gram_far)
    inverse = lax.optimization_barrier(inverse + to_other_core(inverse))

    sum_far = to_other_core(sum_near)
    a_near = jnp.dot(sum_near, inverse, precision=HIGHEST)
    squares = jnp.sum(a_near * a_near, axis=0, keepdims=True)
    squares = squares + along_groups(squares, 1) + along_groups(squares, 2) + along_groups(squares, 3)
    squares = squares + to_other_core(squares)
    a_far = jnp.dot(sum_far, inverse, precision=HIGHEST)
    gram_core = jnp.dot(a_near.T, a_near, precision=HIGHEST)
    gram_plane = gram_core + to_other_core(gram_core)
    gram_parts = [gram_plane] + [along_groups(gram_plane, q) for q in (1, 2, 3)]

    *sends, a_table = mode_two(True, order_two, blocks, pieces, [a_near, a_far, squares])
    gram_parts, sends = lax.optimization_barrier((gram_parts, sends))
    second = inverse_of(
        second_inverse_kernel, "second_inverse", meta, *rings, *gram_parts, gram_near, gram_far
    )
    second, a_table = lax.optimization_barrier((second, a_table))
    [keep] = mode_two(False, order_two, blocks, pieces, [a_table])
    a_update = jnp.dot(sum_own, inverse, precision=HIGHEST)
    arrived = [along_groups(value, q + 1) for q, value in enumerate(sends)]
    arrived, keep, second = lax.optimization_barrier((arrived, keep, second))
    second = lax.optimization_barrier(second + to_other_core(second))
    arrived = [value.astype(F32) for value in arrived]
    own_two = keep + arrived[0] + arrived[1] + arrived[2]
    b_update = jnp.dot(own_two, second, precision=HIGHEST)
    return a_update, b_update


def solution(mesh):
    groups, columns = mesh.shape["grp"], mesh.shape["col"]
    side = round((columns // 2) ** 0.5)
    fine = Mesh(mesh.devices.reshape(groups, side, side, 2), ALL)
    row, flat = P(ALL, None), P(ALL)
    return jax.shard_map(
        on_device,
        mesh=fine,
        in_specs=(P(ALL, None, None), flat, flat, flat, flat, row, row),
        out_specs=(row, row),
        check_vma=False,
    )
```

```python
import jax
import jax.numpy as jnp
from jax import lax
from jax.experimental import pallas as pl
from jax.experimental.pallas import tpu as pltpu
from jax.sharding import Mesh
from jax.sharding import PartitionSpec as P

EDGE = 32
GROUP = 8
DEPTH = 4
B_ROWS = 16 * EDGE
C_ROWS = 4 * EDGE
COUNT_ROWS = 16
MODE_COST = pl.CostEstimate(flops=15_000_000_000, bytes_accessed=48_000_000, transcendentals=0)
LAST_PASS_COST = pl.CostEstimate(flops=2_000_000_000, bytes_accessed=6_000_000, transcendentals=0)
INVERSE_COST = pl.CostEstimate(flops=16_000_000_000, bytes_accessed=50_000_000, transcendentals=0)
VMEM_BYTES = 8 << 20
MODE_VMEM_BYTES = 48 << 20
ALL = ("grp", "x", "z", "core")
PLANE = ("x", "z")
CHIPS = ("grp", "x", "z")
F32 = jnp.float32
BF16 = jnp.bfloat16
HIGHEST = lax.Precision.HIGHEST


def invert_four(p):
    inv_det = 1.0 / (p[0][0] * p[1][1] - p[0][1] * p[0][1])
    a00, a01, a11 = p[1][1] * inv_det, -p[0][1] * inv_det, p[0][0] * inv_det
    t00 = a00 * p[0][2] + a01 * p[1][2]
    t01 = a00 * p[0][3] + a01 * p[1][3]
    t10 = a01 * p[0][2] + a11 * p[1][2]
    t11 = a01 * p[0][3] + a11 * p[1][3]
    s00 = p[2][2] - (p[0][2] * t00 + p[1][2] * t10)
    s01 = p[2][3] - (p[0][2] * t01 + p[1][2] * t11)
    s11 = p[3][3] - (p[0][3] * t01 + p[1][3] * t11)
    inv_det = 1.0 / (s00 * s11 - s01 * s01)
    z00, z01, z11 = s11 * inv_det, -s01 * inv_det, s00 * inv_det
    u00, u01 = t00 * z00 + t01 * z01, t00 * z01 + t01 * z11
    u10, u11 = t10 * z00 + t11 * z01, t10 * z01 + t11 * z11
    x00 = a00 + (u00 * t00 + u01 * t01)
    x01 = a01 + (u00 * t10 + u01 * t11)
    x11 = a11 + (u10 * t10 + u11 * t11)
    return [
        [x00, x01, -u00, -u01],
        [x01, x11, -u10, -u11],
        [-u00, -u10, z00, z01],
        [-u01, -u11, z01, z11],
    ]


def invert_block(w):
    n = w.shape[0]
    row = lax.broadcasted_iota(jnp.int32, (n, n), 0)
    col = lax.broadcasted_iota(jnp.int32, (n, n), 1)
    for k in range(0, n, 4):
        cols = [jnp.broadcast_to(w[:, k + q : k + q + 1], (n, n)) for q in range(4)]
        rows = [w[k + q : k + q + 1, :] for q in range(4)]
        pivot = [[cols[b][k + a : k + a + 1, :] for b in range(4)] for a in range(4)]
        inv = invert_four(pivot)
        lane = col[0:1, :]
        fresh = []
        for a in range(4):
            value = (inv[a][0] * rows[0] + inv[a][1] * rows[1]) + (
                inv[a][2] * rows[2] + inv[a][3] * rows[3]
            )
            for b in range(4):
                value = jnp.where(lane == k + b, inv[a][b], value)
            fresh.append(value)
        in_cols = (col >= k) & (col < k + 4)
        in_rows = (row >= k) & (row < k + 4)
        base = jnp.where(in_cols, 0.0, w)
        update = (cols[0] * fresh[0] + cols[1] * fresh[1]) + (
            cols[2] * fresh[2] + cols[3] * fresh[3]
        )
        out = base - update
        for a in range(4):
            out = jnp.where(row == k + a, fresh[a], out)
        w = out
    return w


def tiles_of(matrix):
    across = matrix.shape[1] // 128
    return [
        (r * across + c, slice(r * 8, r * 8 + 8), slice(c * 128, c * 128 + 128))
        for r in range(matrix.shape[0] // 8)
        for c in range(across)
    ]


WIDTH = 64


def scales(matrix):
    n = matrix.shape[0]
    row = lax.broadcasted_iota(jnp.int32, (n, n), 0)
    col = lax.broadcasted_iota(jnp.int32, (n, n), 1)
    diag = jnp.where(row == col, matrix, 0.0)
    return (
        lax.rsqrt(jnp.sum(diag, axis=0, keepdims=True)),
        lax.rsqrt(jnp.sum(diag, axis=1, keepdims=True)),
    )


def eliminate(work, blocks):
    n = work.shape[0]
    row = lax.broadcasted_iota(jnp.int32, (n, n), 0)
    col = lax.broadcasted_iota(jnp.int32, (n, n), 1)
    for b in blocks:
        span = slice(b * WIDTH, (b + 1) * WIDTH)
        block = invert_block(work[span, span])
        rows = jnp.dot(block, work[span, :], precision=HIGHEST, preferred_element_type=F32)
        parts = [jnp.zeros((WIDTH, WIDTH), F32)] * (n // WIDTH)
        parts[b] = block
        padded = jnp.concatenate(parts, axis=1)
        in_block = (col >= b * WIDTH) & (col < (b + 1) * WIDTH)
        rows = jnp.where(in_block[0:WIDTH], padded, rows)
        left = work[:, span]
        left_row = row[:, 0:WIDTH]
        left = jnp.where((left_row >= b * WIDTH) & (left_row < (b + 1) * WIDTH), 0.0, left)
        base = jnp.where(in_block, 0.0, work[...])
        work[...] = base - jnp.dot(left, rows, precision=HIGHEST, preferred_element_type=F32)
        work[span, :] = rows


def takes_turn(meta, ring, other_ring):
    mine, other = jnp.max(ring[...]), jnp.max(other_ring[...])
    return (mine < other) | ((mine == other) & (meta[2] == 0))


def first_inverse_start_kernel(meta, ring, other_ring, near, far, work):
    @pl.when(takes_turn(meta, ring, other_ring))
    def _():
        for t, rows, cols in tiles_of(work):
            work[rows, cols] = near[t] * far[t]
        scale_row, scale_col = scales(work[...])
        work[...] = work[...] * scale_row * scale_col
        eliminate(work, [0])


def first_inverse_end_kernel(meta, ring, other_ring, near, far, begun, out, work):
    mine = takes_turn(meta, ring, other_ring)

    @pl.when(jnp.logical_not(mine))
    def _():
        out[...] = jnp.zeros_like(out)

    @pl.when(mine)
    def _():
        for t, rows, cols in tiles_of(out):
            out[rows, cols] = near[t] * far[t]
        scale_row, scale_col = scales(out[...])
        work[...] = begun[...]
        eliminate(work, range(1, work.shape[0] // WIDTH))
        out[...] = work[...] * scale_row * scale_col


def second_inverse_kernel(
    meta, ring, other_ring, part_0, part_1, part_2, part_3, near, far, out, work
):
    n = work.shape[0]
    mine = takes_turn(meta, ring, other_ring)

    @pl.when(jnp.logical_not(mine))
    def _():
        out[...] = jnp.zeros_like(out)

    @pl.when(mine)
    def _():
        gram = (part_0[...] + part_1[...]) + (part_2[...] + part_3[...])
        row = lax.broadcasted_iota(jnp.int32, (n, n), 0)
        col = lax.broadcasted_iota(jnp.int32, (n, n), 1)
        diag = jnp.where(row == col, gram, 0.0)
        norm_row = jnp.sqrt(jnp.sum(diag, axis=0, keepdims=True) + 1e-06)
        norm_col = jnp.sqrt(jnp.sum(diag, axis=1, keepdims=True) + 1e-06)
        work[...] = gram / (norm_col * norm_row)
        third_is_near = meta[2] == 1
        for t, rows, cols in tiles_of(work):
            work[rows, cols] = work[rows, cols] * jnp.where(third_is_near, near[t], far[t])
        scale_row, scale_col = scales(work[...])
        work[...] = work[...] * scale_row * scale_col
        eliminate(work, range(n // WIDTH))
        out[...] = work[...] * scale_row * scale_col


def inverse_of(kernel, name, meta, *arrays, scratch=1):
    n = 256
    return pl.pallas_call(
        kernel,
        out_shape=jax.ShapeDtypeStruct((n, n), F32),
        in_specs=[pl.BlockSpec(memory_space=pltpu.SMEM)]
        + [pl.BlockSpec(memory_space=pltpu.VMEM)] * len(arrays),
        out_specs=pl.BlockSpec(memory_space=pltpu.VMEM),
        scratch_shapes=[pltpu.VMEM((n, n), F32)] * scratch,
        compiler_params=pltpu.CompilerParams(vmem_limit_bytes=VMEM_BYTES),
        cost_estimate=INVERSE_COST,
        name=name,
    )(meta, *arrays)


def solve_kernel(sums, inverse_0, inverse_1, solved, squares, gram, inverse):
    inverse[...] = inverse_0[...] + inverse_1[...]
    rows = jnp.dot(sums[...], inverse[...], precision=HIGHEST, preferred_element_type=F32)
    solved[...] = rows
    squares[...] = jnp.sum(rows * rows, axis=0, keepdims=True)
    gram[...] = lax.dot_general(
        rows, rows, (((0,), (0,)), ((), ())), precision=HIGHEST, preferred_element_type=F32
    )


def solve(sums, inverse_0, inverse_1):
    rank = sums.shape[1]
    square = jax.ShapeDtypeStruct((rank, rank), F32)
    return pl.pallas_call(
        solve_kernel,
        out_shape=[
            jax.ShapeDtypeStruct(sums.shape, F32),
            jax.ShapeDtypeStruct((1, rank), F32),
            square,
            square,
        ],
        compiler_params=pltpu.CompilerParams(vmem_limit_bytes=2 * VMEM_BYTES),
        name="solve",
    )(sums, inverse_0, inverse_1)


def prepare_kernel(meta, b_factor, c_factor, own, gram_keep, gram_send):
    rows = b_factor.shape[0]
    core = meta[2]
    own[0:rows, :] = b_factor[...].astype(BF16)
    own[rows : rows + C_ROWS, :] = c_factor[...].astype(BF16)
    count = meta[0].astype(F32)
    own[rows + C_ROWS :, :] = jnp.full((COUNT_ROWS, own.shape[1]), count, F32).astype(BF16)
    for q, ref in enumerate((b_factor, c_factor)):
        gram = lax.dot_general(
            ref[...],
            ref[...],
            (((0,), (0,)), ((), ())),
            precision=HIGHEST,
            preferred_element_type=F32,
        )

        @pl.when(core == q)
        def _():
            for t, r, c in tiles_of(gram):
                gram_keep[t] = gram[r, c]

        @pl.when(core != q)
        def _():
            for t, r, c in tiles_of(gram):
                gram_send[t] = gram[r, c]


def prepare(meta, b_factor, c_factor):
    rank = b_factor.shape[1]
    rows = b_factor.shape[0] + c_factor.shape[0] + COUNT_ROWS
    tiles = jax.ShapeDtypeStruct((rank * rank // 1024, 8, 128), F32)
    return pl.pallas_call(
        prepare_kernel,
        out_shape=[jax.ShapeDtypeStruct((rows, rank), BF16), tiles, tiles],
        grid_spec=pltpu.PrefetchScalarGridSpec(
            num_scalar_prefetch=1,
            grid=(1,),
            in_specs=[
                pl.BlockSpec(b_factor.shape, lambda step, meta: (0, 0)),
                pl.BlockSpec(c_factor.shape, lambda step, meta: (0, 0)),
            ],
            out_specs=[
                pl.BlockSpec((rows, rank), lambda step, meta: (0, 0)),
                pl.BlockSpec(tiles.shape, lambda step, meta: (0, 0, 0)),
                pl.BlockSpec(tiles.shape, lambda step, meta: (0, 0, 0)),
            ],
        ),
        compiler_params=pltpu.CompilerParams(vmem_limit_bytes=2 * VMEM_BYTES),
        name="prepare",
    )(meta, b_factor, c_factor)


def order_kernel(meta, i_idx, j_idx, k_idx, order_one, order_two):
    slots = i_idx.shape[0]
    count, grp, core = meta[0], meta[1], meta[2]

    def place(s, front_one, front_two, i, j, k):
        entry = s + 256 * (i + 64 * (j + 64 * k))
        one = ((i >> 1) & 1) ^ core
        two = jnp.where((j >> 4) == grp, 0, 1)
        order_one[jnp.where(one == 1, front_one, slots - 1 - (s - front_one))] = entry
        order_two[jnp.where(two == 1, front_two, slots - 1 - (s - front_two))] = entry
        return front_one + one, front_two + two

    def place_four(q, carry):
        found = [(i_idx[4 * q + u], j_idx[4 * q + u], k_idx[4 * q + u]) for u in range(4)]
        for u in range(4):
            carry = place(4 * q + u, *carry, *found[u])
        return carry

    def place_one(s, carry):
        return place(s, *carry, i_idx[s], j_idx[s], k_idx[s])

    zero = (jnp.int32(0), jnp.int32(0))
    fours = count // 4
    ends = lax.fori_loop(4 * fours, count, place_one, lax.fori_loop(0, fours, place_four, zero))
    for order, front in zip((order_one, order_two), ends):
        order[slots] = front
        order[slots + 1] = count - front
        order[slots + 2] = grp
        order[slots + 3] = core


def order_slots(meta, i_index, j_index, k_index):
    table = jax.ShapeDtypeStruct((i_index.shape[0] + 64,), jnp.int32)
    smem = pl.BlockSpec(memory_space=pltpu.SMEM)
    return pl.pallas_call(
        order_kernel,
        out_shape=[table] * 2,
        in_specs=[smem] * 4,
        out_specs=[smem] * 2,
        name="order_slots",
    )(meta, i_index, j_index, k_index)


def block_rows(ref, start):
    return ref[pl.ds(pl.multiple_of(start, EDGE), EDGE), :]


def copy_all(copies):
    for copy in copies:
        copy.start()
    return copies


def wait_all(copies):
    for copy in copies:
        copy.wait()


def for_each_group(first, order, blocks, buffer, sems, prepare_tables, one_slot):
    slots = blocks.shape[0]
    count = order[slots if first else slots + 1]
    groups = (count + GROUP - 1) // GROUP

    def entry_at(place):
        place = jnp.minimum(place, count - 1)
        return order[place if first else slots - 1 - place]

    def copies(group):
        side = group & (DEPTH - 1)
        return [
            pltpu.make_async_copy(
                blocks.at[entry_at(group * GROUP + u) & 255], buffer.at[side, u], sems.at[side, u]
            )
            for u in range(GROUP)
        ]

    for ahead in range(DEPTH - 1):

        @pl.when(ahead < groups)
        def _():
            copy_all(copies(ahead))

    prepare_tables()

    def one_group(group, carry):
        @pl.when(group + DEPTH - 1 < groups)
        def _():
            copy_all(copies(group + DEPTH - 1))

        wait_all(copies(group))
        for u in range(GROUP):
            place = group * GROUP + u
            entry = entry_at(place)
            i, j, k = (entry >> 8) & 63, (entry >> 14) & 63, (entry >> 20) & 15
            one_slot(buffer[group & (DEPTH - 1), u], u, i, j, k, place < count)
        return carry

    lax.fori_loop(0, groups, one_group, 0)


def mode_one_kernel(
    first, order, blocks, own_0, own_1, own_2, own_3, out, *rest
):
    ring = rest[0] if first else None
    buffer, table, acc, sems, table_sems = rest[-5:]
    grp = order[blocks.shape[0] + 2]
    own = own_0.shape[0]
    half = out.shape[0]

    def prepare_tables():
        pieces = copy_all(
            [
                pltpu.make_async_copy(ref, table.at[pl.ds(q * own, own)], table_sems.at[q])
                for q, ref in enumerate((own_0, own_1, own_2, own_3))
            ]
        )
        acc[...] = jnp.zeros_like(acc)
        wait_all(pieces)

    def one_slot(block, u, i, j, k, live):
        b_rows = block_rows(table, ((grp - (j >> 4)) & 3) * own + (j & 15) * EDGE)
        c_rows = block_rows(table, ((grp - (k >> 2)) & 3) * own + B_ROWS + (k & 3) * EDGE)
        product = (b_rows[:, None, :] * c_rows[None, :, :]).reshape(EDGE * EDGE, -1)
        result = jnp.dot(block, product, preferred_element_type=F32)
        target = jnp.where(live, (i >> 2) * (2 * EDGE) + (i & 1) * EDGE, half)
        acc[pl.ds(pl.multiple_of(target, EDGE), EDGE), :] += result

    for_each_group(first, order, blocks, buffer, sems, prepare_tables, one_slot)
    out[...] = acc[0:half, :]
    if first:
        counts = [
            table[(q + 1) * own - COUNT_ROWS : (q + 1) * own, 0:128].astype(F32) for q in range(4)
        ]
        most = jnp.maximum(jnp.maximum(counts[0], counts[1]), jnp.maximum(counts[2], counts[3]))
        ring[...] = most[0:8, :]


def turn_block(block, turned, u):
    lane = lax.broadcasted_iota(jnp.int32, (8, 128), 1)
    low_half = lane < 64
    even_group = (lane // 32) % 2 == 0
    wide = block.astype(F32)
    for jh in range(8):
        t = [wide[il * 8 : il * 8 + 8, jh * 128 : jh * 128 + 128] for il in range(4)]
        m = [None] * 4
        for il in range(2):
            m[il] = jnp.where(low_half, t[il], pltpu.roll(t[il + 2], 64, 1))
            m[il + 2] = jnp.where(low_half, pltpu.roll(t[il], 64, 1), t[il + 2])
        for q in (0, 2):
            j = jh * 4 + q
            turned[u, j * 8 : j * 8 + 8, :] = jnp.where(
                even_group, m[q], pltpu.roll(m[q + 1], 32, 1)
            )
            turned[u, j * 8 + 8 : j * 8 + 16, :] = jnp.where(
                even_group, pltpu.roll(m[q], 96, 1), m[q + 1]
            )
    return jnp.concatenate(
        [turned[u, pl.ds(ih, EDGE, stride=8), :].astype(BF16) for ih in range(8)], axis=1
    )


def mode_two_slots(first, order, blocks, owns, a_table, scratch, part):
    buffer, turned, table, acc, sems, table_sems = scratch
    grp, core = order[blocks.shape[0] + 2], order[blocks.shape[0] + 3]
    half = a_table.shape[0] // 2

    def prepare_tables():
        pieces = copy_all(
            [
                pltpu.make_async_copy(
                    ref.at[pl.ds(B_ROWS, C_ROWS)],
                    table.at[pl.ds(q * C_ROWS, C_ROWS)],
                    table_sems.at[q],
                )
                for q, ref in enumerate(owns)
            ]
        )
        acc[...] = jnp.zeros_like(acc)
        wait_all(pieces)

    def one_slot(block, u, i, j, k, live):
        a_rows = block_rows(
            a_table,
            (((i >> 1) & 1) ^ core) * half + (i >> 2) * (2 * EDGE) + (i & 1) * EDGE,
        )
        c_rows = block_rows(table, ((grp - (k >> 2)) & 3) * C_ROWS + (k & 3) * EDGE)
        left = turn_block(block, turned, u)
        product = jnp.concatenate(
            [
                a_rows[il * 8 + ih : il * 8 + ih + 1, :] * c_rows
                for ih in range(8)
                for il in range(4)
            ],
            axis=0,
        )
        result = jnp.dot(left, product, preferred_element_type=F32)
        target = (j & 15) * EDGE
        if first:
            target += (((j >> 4) - grp - 1) & 3) * part
        target = jnp.where(live, target, acc.shape[0] - EDGE)
        acc[pl.ds(pl.multiple_of(target, EDGE), EDGE), :] += result

    for_each_group(first, order, blocks, buffer, sems, prepare_tables, one_slot)


def mode_two_others_kernel(
    order,
    blocks,
    own_0,
    own_1,
    own_2,
    own_3,
    a_near,
    a_far,
    squares,
    send_1,
    send_2,
    send_3,
    a_table,
    *scratch,
):
    half = a_near.shape[0]
    part = send_1.shape[0]
    inv_norm = 1.0 / jnp.sqrt(squares[...] + 1e-06)
    a_table[0:half, :] = (a_near[...] * inv_norm).astype(BF16)
    a_table[half : 2 * half, :] = (a_far[...] * inv_norm).astype(BF16)
    mode_two_slots(True, order, blocks, (own_0, own_1, own_2, own_3), a_table, scratch, part)
    acc = scratch[3]
    for q, ref in enumerate((send_1, send_2, send_3)):
        ref[...] = acc[q * part : (q + 1) * part, :].astype(BF16)


def mode_two_own_kernel(order, blocks, own_0, own_1, own_2, own_3, a_table, keep, *scratch):
    part = keep.shape[0]
    mode_two_slots(False, order, blocks, (own_0, own_1, own_2, own_3), a_table, scratch, part)
    keep[...] = scratch[3][0:part, :]


def mode_call(kernel, name, order, in_place, resident, out_shape, scratch):
    smem, anywhere, vmem = (
        pl.BlockSpec(memory_space=pltpu.SMEM),
        pl.BlockSpec(memory_space=pl.ANY),
        pl.BlockSpec(memory_space=pltpu.VMEM),
    )
    blocks = in_place[0]
    buffer = pltpu.VMEM((DEPTH, GROUP) + blocks.shape[1:], blocks.dtype)
    return pl.pallas_call(
        kernel,
        out_shape=out_shape,
        in_specs=[smem] + [anywhere] * len(in_place) + [vmem] * len(resident),
        out_specs=[vmem] * len(out_shape),
        scratch_shapes=[buffer]
        + scratch
        + [pltpu.SemaphoreType.DMA((DEPTH, GROUP)), pltpu.SemaphoreType.DMA((4,))],
        compiler_params=pltpu.CompilerParams(vmem_limit_bytes=MODE_VMEM_BYTES),
        cost_estimate=LAST_PASS_COST if name == "mode_two_own_group" else MODE_COST,
        name=name,
    )(order, *in_place, *resident)


def mode_one(first, order, blocks, pieces):
    own, rank = pieces[0].shape
    half = 32 * EDGE

    def kernel(*refs):
        mode_one_kernel(first, *refs)

    return mode_call(
        kernel,
        "mode_one_other_core" if first else "mode_one_own_core",
        order,
        [blocks] + pieces,
        [],
        [jax.ShapeDtypeStruct((half, rank), F32)]
        + ([jax.ShapeDtypeStruct((8, 128), F32)] if first else []),
        [pltpu.VMEM((4 * own, rank), BF16), pltpu.VMEM((half + EDGE, rank), F32)],
    )


def mode_two(first, order, blocks, pieces, resident):
    rank = pieces[0].shape[1]
    part = 16 * EDGE
    sent = jax.ShapeDtypeStruct((part, rank), BF16)
    if first:
        out_shape = [sent] * 3 + [jax.ShapeDtypeStruct((64 * EDGE, rank), BF16)]
    else:
        out_shape = [jax.ShapeDtypeStruct((part, rank), F32)]
    return mode_call(
        mode_two_others_kernel if first else mode_two_own_kernel,
        "mode_two_other_groups" if first else "mode_two_own_group",
        order,
        [blocks] + pieces,
        resident,
        out_shape,
        [
            pltpu.VMEM((GROUP, 8 * EDGE, 128), F32),
            pltpu.VMEM((4 * C_ROWS, rank), BF16),
            pltpu.VMEM(((3 if first else 1) * part + EDGE, rank), F32),
        ],
    )


def to_other_core(value):
    return lax.ppermute(value, "core", [(0, 1), (1, 0)])


def along_groups(value, shift):
    size = lax.axis_size("grp")
    return lax.ppermute(value, "grp", [(p, (p + shift) % size) for p in range(size)])


def exchange(value, axes):
    return lax.all_to_all(value, axes, 0, 0)


def on_device(blocks, i_index, j_index, k_index, block_count, b_factor, c_factor):
    rank = b_factor.shape[1]
    grp, core = lax.axis_index("grp"), lax.axis_index("core")
    plane = lax.axis_size(PLANE)
    chips = lax.axis_size(CHIPS)
    meta = jnp.stack([block_count[0], grp, core])

    own, gram_keep, gram_send = prepare(meta, b_factor, c_factor)
    gram_pair = gram_keep + to_other_core(gram_send)
    gram_pair, late_meta = lax.optimization_barrier((gram_pair, meta))
    order_one, order_two = order_slots(late_meta, i_index, j_index, k_index)
    pieces = [own] + [along_groups(own, q) for q in (1, 2, 3)]
    gram_parts = exchange(gram_pair.reshape(chips, -1, 8, 128), CHIPS)
    send, ring = mode_one(True, order_one, blocks, pieces)
    piece = jnp.sum(gram_parts, axis=0)
    piece, send = lax.optimization_barrier((piece, send))
    spread = jnp.broadcast_to(piece[None], (chips,) + piece.shape)
    spread, pieces = lax.optimization_barrier((spread, pieces))
    gram_near = exchange(spread, CHIPS)
    [keep] = mode_one(False, order_one, blocks, pieces)
    gram_near, keep = lax.optimization_barrier((gram_near, keep))
    gram_near = gram_near.reshape(-1, 8, 128)
    gram_far = to_other_core(gram_near)
    rings = (ring, to_other_core(ring))

    pair_sum = (keep + to_other_core(send)).astype(BF16)
    arrived = exchange(pair_sum.reshape(plane, -1, rank), PLANE)
    begun = inverse_of(
        first_inverse_start_kernel, "first_inverse_start", meta, *rings, gram_near, gram_far, scratch=0
    )
    begun, arrived = lax.optimization_barrier((begun, arrived))
    sum_own = jnp.sum(arrived.astype(F32), axis=0)
    sum_near = exchange(jnp.broadcast_to(sum_own[None], (plane,) + sum_own.shape), PLANE)
    sum_near = sum_near.reshape(-1, rank)

    inverse = inverse_of(
        first_inverse_end_kernel, "first_inverse_end", meta, *rings, gram_near, gram_far, begun
    )
    inverse, sum_near = lax.optimization_barrier((inverse, sum_near))
    sum_far = to_other_core(sum_near)
    a_near, squares, gram_core, inverse = solve(sum_near, inverse, to_other_core(inverse))
    squares = squares + along_groups(squares, 1) + along_groups(squares, 2) + along_groups(squares, 3)
    squares = squares + to_other_core(squares)
    a_far = jnp.dot(sum_far, inverse, precision=HIGHEST)
    gram_plane = gram_core + to_other_core(gram_core)
    gram_parts = [gram_plane] + [along_groups(gram_plane, q) for q in (1, 2, 3)]

    *sends, a_table = mode_two(True, order_two, blocks, pieces, [a_near, a_far, squares])
    gram_parts, sends = lax.optimization_barrier((gram_parts, sends))
    second = inverse_of(
        second_inverse_kernel, "second_inverse", meta, *rings, *gram_parts, gram_near, gram_far
    )
    second, a_table = lax.optimization_barrier((second, a_table))
    [keep] = mode_two(False, order_two, blocks, pieces, [a_table])
    a_update = jnp.dot(sum_own, inverse, precision=HIGHEST)
    arrived = [along_groups(value, q + 1) for q, value in enumerate(sends)]
    arrived, keep, second = lax.optimization_barrier((arrived, keep, second))
    second = lax.optimization_barrier(second + to_other_core(second))
    arrived = [value.astype(F32) for value in arrived]
    own_two = keep + arrived[0] + arrived[1] + arrived[2]
    b_update = jnp.dot(own_two, second, precision=HIGHEST)
    return a_update, b_update


def solution(mesh):
    groups, columns = mesh.shape["grp"], mesh.shape["col"]
    side = round((columns // 2) ** 0.5)
    fine = Mesh(mesh.devices.reshape(groups, side, side, 2), ALL)
    row, flat = P(ALL, None), P(ALL)
    return jax.shard_map(
        on_device,
        mesh=fine,
        in_specs=(P(ALL, None, None), flat, flat, flat, flat, row, row),
        out_specs=(row, row),
        check_vma=False,
    )
```

```python
import jax
import jax.numpy as jnp
from jax import lax
from jax.experimental import pallas as pl
from jax.experimental.pallas import tpu as pltpu
from jax.sharding import Mesh
from jax.sharding import PartitionSpec as P

EDGE = 32
GROUP = 8
DEPTH = 4
B_ROWS = 16 * EDGE
C_ROWS = 4 * EDGE
COUNT_ROWS = 16
MODE_COST = pl.CostEstimate(flops=15_000_000_000, bytes_accessed=48_000_000, transcendentals=0)
LAST_PASS_COST = pl.CostEstimate(flops=2_000_000_000, bytes_accessed=6_000_000, transcendentals=0)
INVERSE_COST = pl.CostEstimate(flops=16_000_000_000, bytes_accessed=50_000_000, transcendentals=0)
VMEM_BYTES = 8 << 20
MODE_VMEM_BYTES = 48 << 20
ALL = ("grp", "x", "z", "core")
PLANE = ("x", "z")
CHIPS = ("grp", "x", "z")
F32 = jnp.float32
BF16 = jnp.bfloat16
HIGHEST = lax.Precision.HIGHEST


def invert_four(p):
    inv_det = 1.0 / (p[0][0] * p[1][1] - p[0][1] * p[0][1])
    a00, a01, a11 = p[1][1] * inv_det, -p[0][1] * inv_det, p[0][0] * inv_det
    t00 = a00 * p[0][2] + a01 * p[1][2]
    t01 = a00 * p[0][3] + a01 * p[1][3]
    t10 = a01 * p[0][2] + a11 * p[1][2]
    t11 = a01 * p[0][3] + a11 * p[1][3]
    s00 = p[2][2] - (p[0][2] * t00 + p[1][2] * t10)
    s01 = p[2][3] - (p[0][2] * t01 + p[1][2] * t11)
    s11 = p[3][3] - (p[0][3] * t01 + p[1][3] * t11)
    inv_det = 1.0 / (s00 * s11 - s01 * s01)
    z00, z01, z11 = s11 * inv_det, -s01 * inv_det, s00 * inv_det
    u00, u01 = t00 * z00 + t01 * z01, t00 * z01 + t01 * z11
    u10, u11 = t10 * z00 + t11 * z01, t10 * z01 + t11 * z11
    x00 = a00 + (u00 * t00 + u01 * t01)
    x01 = a01 + (u00 * t10 + u01 * t11)
    x11 = a11 + (u10 * t10 + u11 * t11)
    return [
        [x00, x01, -u00, -u01],
        [x01, x11, -u10, -u11],
        [-u00, -u10, z00, z01],
        [-u01, -u11, z01, z11],
    ]


def invert_block(w):
    n = w.shape[0]
    row = lax.broadcasted_iota(jnp.int32, (n, n), 0)
    col = lax.broadcasted_iota(jnp.int32, (n, n), 1)
    for k in range(0, n, 4):
        cols = [jnp.broadcast_to(w[:, k + q : k + q + 1], (n, n)) for q in range(4)]
        rows = [w[k + q : k + q + 1, :] for q in range(4)]
        pivot = [[cols[b][k + a : k + a + 1, :] for b in range(4)] for a in range(4)]
        inv = invert_four(pivot)
        lane = col[0:1, :]
        fresh = []
        for a in range(4):
            value = (inv[a][0] * rows[0] + inv[a][1] * rows[1]) + (
                inv[a][2] * rows[2] + inv[a][3] * rows[3]
            )
            for b in range(4):
                value = jnp.where(lane == k + b, inv[a][b], value)
            fresh.append(value)
        in_cols = (col >= k) & (col < k + 4)
        in_rows = (row >= k) & (row < k + 4)
        base = jnp.where(in_cols, 0.0, w)
        update = (cols[0] * fresh[0] + cols[1] * fresh[1]) + (
            cols[2] * fresh[2] + cols[3] * fresh[3]
        )
        out = base - update
        for a in range(4):
            out = jnp.where(row == k + a, fresh[a], out)
        w = out
    return w


def tiles_of(matrix):
    across = matrix.shape[1] // 128
    return [
        (r * across + c, slice(r * 8, r * 8 + 8), slice(c * 128, c * 128 + 128))
        for r in range(matrix.shape[0] // 8)
        for c in range(across)
    ]


def invert(out, work):
    n = work.shape[0]
    width = 64
    row = lax.broadcasted_iota(jnp.int32, (n, n), 0)
    col = lax.broadcasted_iota(jnp.int32, (n, n), 1)
    diag = jnp.where(row == col, work[...], 0.0)
    scale_row = lax.rsqrt(jnp.sum(diag, axis=0, keepdims=True))
    scale_col = lax.rsqrt(jnp.sum(diag, axis=1, keepdims=True))
    work[...] = work[...] * scale_row * scale_col
    for b in range(n // width):
        span = slice(b * width, (b + 1) * width)
        block = invert_block(work[span, span])
        rows = jnp.dot(block, work[span, :], precision=HIGHEST, preferred_element_type=F32)
        parts = [jnp.zeros((width, width), F32)] * (n // width)
        parts[b] = block
        padded = jnp.concatenate(parts, axis=1)
        in_block = (col >= b * width) & (col < (b + 1) * width)
        rows = jnp.where(in_block[0:width], padded, rows)
        left = work[:, span]
        left_row = row[:, 0:width]
        left = jnp.where((left_row >= b * width) & (left_row < (b + 1) * width), 0.0, left)
        base = jnp.where(in_block, 0.0, work[...])
        work[...] = base - jnp.dot(left, rows, precision=HIGHEST, preferred_element_type=F32)
        work[span, :] = rows
    out[...] = work[...] * scale_row * scale_col


def takes_turn(meta, ring, other_ring):
    mine, other = jnp.max(ring[...]), jnp.max(other_ring[...])
    return (mine < other) | ((mine == other) & (meta[2] == 0))


def first_inverse_kernel(meta, ring, other_ring, near, far, out, work):
    mine = takes_turn(meta, ring, other_ring)

    @pl.when(jnp.logical_not(mine))
    def _():
        out[...] = jnp.zeros_like(out)

    @pl.when(mine)
    def _():
        for t, rows, cols in tiles_of(work):
            work[rows, cols] = near[t] * far[t]
        invert(out, work)


def second_inverse_kernel(
    meta, ring, other_ring, part_0, part_1, part_2, part_3, near, far, out, work
):
    n = work.shape[0]
    mine = takes_turn(meta, ring, other_ring)

    @pl.when(jnp.logical_not(mine))
    def _():
        out[...] = jnp.zeros_like(out)

    @pl.when(mine)
    def _():
        gram = (part_0[...] + part_1[...]) + (part_2[...] + part_3[...])
        row = lax.broadcasted_iota(jnp.int32, (n, n), 0)
        col = lax.broadcasted_iota(jnp.int32, (n, n), 1)
        diag = jnp.where(row == col, gram, 0.0)
        norm_row = jnp.sqrt(jnp.sum(diag, axis=0, keepdims=True) + 1e-06)
        norm_col = jnp.sqrt(jnp.sum(diag, axis=1, keepdims=True) + 1e-06)
        work[...] = gram / (norm_col * norm_row)
        third_is_near = meta[2] == 1
        for t, rows, cols in tiles_of(work):
            work[rows, cols] = work[rows, cols] * jnp.where(third_is_near, near[t], far[t])
        invert(out, work)


def inverse_of(kernel, name, meta, *arrays):
    n = 256
    return pl.pallas_call(
        kernel,
        out_shape=jax.ShapeDtypeStruct((n, n), F32),
        in_specs=[pl.BlockSpec(memory_space=pltpu.SMEM)]
        + [pl.BlockSpec(memory_space=pltpu.VMEM)] * len(arrays),
        out_specs=pl.BlockSpec(memory_space=pltpu.VMEM),
        scratch_shapes=[pltpu.VMEM((n, n), F32)],
        compiler_params=pltpu.CompilerParams(vmem_limit_bytes=VMEM_BYTES),
        cost_estimate=INVERSE_COST,
        name=name,
    )(meta, *arrays)


def solve_kernel(near, far, inverse_0, inverse_1, solved_near, solved_far, squares, gram, inverse):
    inverse[...] = inverse_0[...] + inverse_1[...]
    solved_far[...] = jnp.dot(
        far[...], inverse[...], precision=HIGHEST, preferred_element_type=F32
    )
    rows = jnp.dot(near[...], inverse[...], precision=HIGHEST, preferred_element_type=F32)
    solved_near[...] = rows
    squares[...] = jnp.sum(rows * rows, axis=0, keepdims=True)
    gram[...] = lax.dot_general(
        rows, rows, (((0,), (0,)), ((), ())), precision=HIGHEST, preferred_element_type=F32
    )


def solve(near, far, inverse_0, inverse_1):
    rank = near.shape[1]
    rows, square = jax.ShapeDtypeStruct(near.shape, F32), jax.ShapeDtypeStruct((rank, rank), F32)
    return pl.pallas_call(
        solve_kernel,
        out_shape=[rows, rows, jax.ShapeDtypeStruct((1, rank), F32), square, square],
        compiler_params=pltpu.CompilerParams(vmem_limit_bytes=2 * VMEM_BYTES),
        name="solve",
    )(near, far, inverse_0, inverse_1)


def prepare_kernel(meta, b_hbm, c_hbm, own, gram_keep, gram_send, b_factor, c_factor, sems):
    rows = b_factor.shape[0]
    core = meta[2]
    wait_all(
        copy_all(
            [
                pltpu.make_async_copy(b_hbm, b_factor, sems.at[0]),
                pltpu.make_async_copy(c_hbm, c_factor, sems.at[1]),
            ]
        )
    )
    own[0:rows, :] = b_factor[...].astype(BF16)
    own[rows : rows + C_ROWS, :] = c_factor[...].astype(BF16)
    count = meta[0].astype(F32)
    own[rows + C_ROWS :, :] = jnp.full((COUNT_ROWS, own.shape[1]), count, F32).astype(BF16)
    for q, ref in enumerate((b_factor, c_factor)):
        gram = lax.dot_general(
            ref[...],
            ref[...],
            (((0,), (0,)), ((), ())),
            precision=HIGHEST,
            preferred_element_type=F32,
        )

        @pl.when(core == q)
        def _():
            for t, r, c in tiles_of(gram):
                gram_keep[t] = gram[r, c]

        @pl.when(core != q)
        def _():
            for t, r, c in tiles_of(gram):
                gram_send[t] = gram[r, c]


def prepare(meta, b_factor, c_factor):
    rank = b_factor.shape[1]
    rows = b_factor.shape[0] + c_factor.shape[0] + COUNT_ROWS
    tiles = jax.ShapeDtypeStruct((rank * rank // 1024, 8, 128), F32)
    return pl.pallas_call(
        prepare_kernel,
        out_shape=[jax.ShapeDtypeStruct((rows, rank), BF16), tiles, tiles],
        in_specs=[pl.BlockSpec(memory_space=pltpu.SMEM)]
        + [pl.BlockSpec(memory_space=pl.ANY)] * 2,
        scratch_shapes=[
            pltpu.VMEM(b_factor.shape, F32),
            pltpu.VMEM(c_factor.shape, F32),
            pltpu.SemaphoreType.DMA((2,)),
        ],
        compiler_params=pltpu.CompilerParams(vmem_limit_bytes=VMEM_BYTES),
        name="prepare",
    )(meta, b_factor, c_factor)


def order_kernel(meta, i_idx, j_idx, k_idx, order_one, order_two):
    slots = i_idx.shape[0]
    count, grp, core = meta[0], meta[1], meta[2]

    def place(s, front_one, front_two, i, j, k):
        entry = s + 256 * (i + 64 * (j + 64 * k))
        one = ((i >> 1) & 1) ^ core
        two = jnp.where((j >> 4) == grp, 0, 1)
        order_one[jnp.where(one == 1, front_one, slots - 1 - (s - front_one))] = entry
        order_two[jnp.where(two == 1, front_two, slots - 1 - (s - front_two))] = entry
        return front_one + one, front_two + two

    def place_four(q, carry):
        found = [(i_idx[4 * q + u], j_idx[4 * q + u], k_idx[4 * q + u]) for u in range(4)]
        for u in range(4):
            carry = place(4 * q + u, *carry, *found[u])
        return carry

    def place_one(s, carry):
        return place(s, *carry, i_idx[s], j_idx[s], k_idx[s])

    zero = (jnp.int32(0), jnp.int32(0))
    fours = count // 4
    ends = lax.fori_loop(4 * fours, count, place_one, lax.fori_loop(0, fours, place_four, zero))
    for order, front in zip((order_one, order_two), ends):
        order[slots] = front
        order[slots + 1] = count - front
        order[slots + 2] = grp
        order[slots + 3] = core


def order_slots(meta, i_index, j_index, k_index):
    table = jax.ShapeDtypeStruct((i_index.shape[0] + 64,), jnp.int32)
    smem = pl.BlockSpec(memory_space=pltpu.SMEM)
    return pl.pallas_call(
        order_kernel,
        out_shape=[table] * 2,
        in_specs=[smem] * 4,
        out_specs=[smem] * 2,
        name="order_slots",
    )(meta, i_index, j_index, k_index)


def block_rows(ref, start):
    return ref[pl.ds(pl.multiple_of(start, EDGE), EDGE), :]


def copy_all(copies):
    for copy in copies:
        copy.start()
    return copies


def wait_all(copies):
    for copy in copies:
        copy.wait()


def for_each_group(first, order, blocks, buffer, sems, prepare_tables, one_slot):
    slots = blocks.shape[0]
    count = order[slots if first else slots + 1]
    groups = (count + GROUP - 1) // GROUP

    def entry_at(place):
        place = jnp.minimum(place, count - 1)
        return order[place if first else slots - 1 - place]

    def copies(group):
        side = group & (DEPTH - 1)
        return [
            pltpu.make_async_copy(
                blocks.at[entry_at(group * GROUP + u) & 255], buffer.at[side, u], sems.at[side, u]
            )
            for u in range(GROUP)
        ]

    for ahead in range(DEPTH - 1):

        @pl.when(ahead < groups)
        def _():
            copy_all(copies(ahead))

    prepare_tables()

    def one_group(group, carry):
        @pl.when(group + DEPTH - 1 < groups)
        def _():
            copy_all(copies(group + DEPTH - 1))

        wait_all(copies(group))
        for u in range(GROUP):
            place = group * GROUP + u
            entry = entry_at(place)
            i, j, k = (entry >> 8) & 63, (entry >> 14) & 63, (entry >> 20) & 15
            one_slot(buffer[group & (DEPTH - 1), u], u, i, j, k, place < count)
        return carry

    lax.fori_loop(0, groups, one_group, 0)


def mode_one_kernel(
    first, order, blocks, own_0, own_1, own_2, own_3, out, *rest
):
    ring = rest[0] if first else None
    buffer, table, acc, sems, table_sems = rest[-5:]
    grp = order[blocks.shape[0] + 2]
    own = own_0.shape[0]
    half = out.shape[0]

    def prepare_tables():
        pieces = copy_all(
            [
                pltpu.make_async_copy(ref, table.at[pl.ds(q * own, own)], table_sems.at[q])
                for q, ref in enumerate((own_0, own_1, own_2, own_3))
            ]
        )
        acc[...] = jnp.zeros_like(acc)
        wait_all(pieces)

    def one_slot(block, u, i, j, k, live):
        b_rows = block_rows(table, ((grp - (j >> 4)) & 3) * own + (j & 15) * EDGE)
        c_rows = block_rows(table, ((grp - (k >> 2)) & 3) * own + B_ROWS + (k & 3) * EDGE)
        product = (b_rows[:, None, :] * c_rows[None, :, :]).reshape(EDGE * EDGE, -1)
        result = jnp.dot(block, product, preferred_element_type=F32)
        target = jnp.where(live, (i >> 2) * (2 * EDGE) + (i & 1) * EDGE, half)
        acc[pl.ds(pl.multiple_of(target, EDGE), EDGE), :] += result

    for_each_group(first, order, blocks, buffer, sems, prepare_tables, one_slot)
    out[...] = acc[0:half, :]
    if first:
        counts = [
            table[(q + 1) * own - COUNT_ROWS : (q + 1) * own, 0:128].astype(F32) for q in range(4)
        ]
        most = jnp.maximum(jnp.maximum(counts[0], counts[1]), jnp.maximum(counts[2], counts[3]))
        ring[...] = most[0:8, :]


def turn_block(block, turned, u):
    lane = lax.broadcasted_iota(jnp.int32, (8, 128), 1)
    low_half = lane < 64
    even_group = (lane // 32) % 2 == 0
    wide = block.astype(F32)
    for jh in range(8):
        t = [wide[il * 8 : il * 8 + 8, jh * 128 : jh * 128 + 128] for il in range(4)]
        m = [None] * 4
        for il in range(2):
            m[il] = jnp.where(low_half, t[il], pltpu.roll(t[il + 2], 64, 1))
            m[il + 2] = jnp.where(low_half, pltpu.roll(t[il], 64, 1), t[il + 2])
        for q in (0, 2):
            j = jh * 4 + q
            turned[u, j * 8 : j * 8 + 8, :] = jnp.where(
                even_group, m[q], pltpu.roll(m[q + 1], 32, 1)
            )
            turned[u, j * 8 + 8 : j * 8 + 16, :] = jnp.where(
                even_group, pltpu.roll(m[q], 96, 1), m[q + 1]
            )
    return jnp.concatenate(
        [turned[u, pl.ds(ih, EDGE, stride=8), :].astype(BF16) for ih in range(8)], axis=1
    )


def mode_two_slots(first, order, blocks, owns, a_table, scratch, part):
    buffer, turned, table, acc, sems, table_sems = scratch
    grp, core = order[blocks.shape[0] + 2], order[blocks.shape[0] + 3]
    half = a_table.shape[0] // 2

    def prepare_tables():
        pieces = copy_all(
            [
                pltpu.make_async_copy(
                    ref.at[pl.ds(B_ROWS, C_ROWS)],
                    table.at[pl.ds(q * C_ROWS, C_ROWS)],
                    table_sems.at[q],
                )
                for q, ref in enumerate(owns)
            ]
        )
        acc[...] = jnp.zeros_like(acc)
        wait_all(pieces)

    def one_slot(block, u, i, j, k, live):
        a_rows = block_rows(
            a_table,
            (((i >> 1) & 1) ^ core) * half + (i >> 2) * (2 * EDGE) + (i & 1) * EDGE,
        )
        c_rows = block_rows(table, ((grp - (k >> 2)) & 3) * C_ROWS + (k & 3) * EDGE)
        left = turn_block(block, turned, u)
        product = jnp.concatenate(
            [
                a_rows[il * 8 + ih : il * 8 + ih + 1, :] * c_rows
                for ih in range(8)
                for il in range(4)
            ],
            axis=0,
        )
        result = jnp.dot(left, product, preferred_element_type=F32)
        target = (j & 15) * EDGE
        if first:
            target += (((j >> 4) - grp - 1) & 3) * part
        target = jnp.where(live, target, acc.shape[0] - EDGE)
        acc[pl.ds(pl.multiple_of(target, EDGE), EDGE), :] += result

    for_each_group(first, order, blocks, buffer, sems, prepare_tables, one_slot)


def mode_two_others_kernel(
    order,
    blocks,
    own_0,
    own_1,
    own_2,
    own_3,
    a_near,
    a_far,
    squares,
    send_1,
    send_2,
    send_3,
    a_table,
    *scratch,
):
    half = a_near.shape[0]
    part = send_1.shape[0]
    inv_norm = 1.0 / jnp.sqrt(squares[...] + 1e-06)
    a_table[0:half, :] = (a_near[...] * inv_norm).astype(BF16)
    a_table[half : 2 * half, :] = (a_far[...] * inv_norm).astype(BF16)
    mode_two_slots(True, order, blocks, (own_0, own_1, own_2, own_3), a_table, scratch, part)
    acc = scratch[3]
    for q, ref in enumerate((send_1, send_2, send_3)):
        ref[...] = acc[q * part : (q + 1) * part, :].astype(BF16)


def mode_two_own_kernel(order, blocks, own_0, own_1, own_2, own_3, a_table, keep, *scratch):
    part = keep.shape[0]
    mode_two_slots(False, order, blocks, (own_0, own_1, own_2, own_3), a_table, scratch, part)
    keep[...] = scratch[3][0:part, :]


def mode_call(kernel, name, order, in_place, resident, out_shape, scratch):
    smem, anywhere, vmem = (
        pl.BlockSpec(memory_space=pltpu.SMEM),
        pl.BlockSpec(memory_space=pl.ANY),
        pl.BlockSpec(memory_space=pltpu.VMEM),
    )
    blocks = in_place[0]
    buffer = pltpu.VMEM((DEPTH, GROUP) + blocks.shape[1:], blocks.dtype)
    return pl.pallas_call(
        kernel,
        out_shape=out_shape,
        in_specs=[smem] + [anywhere] * len(in_place) + [vmem] * len(resident),
        out_specs=[vmem] * len(out_shape),
        scratch_shapes=[buffer]
        + scratch
        + [pltpu.SemaphoreType.DMA((DEPTH, GROUP)), pltpu.SemaphoreType.DMA((4,))],
        compiler_params=pltpu.CompilerParams(vmem_limit_bytes=MODE_VMEM_BYTES),
        cost_estimate=LAST_PASS_COST if name == "mode_two_own_group" else MODE_COST,
        name=name,
    )(order, *in_place, *resident)


def mode_one(first, order, blocks, pieces):
    own, rank = pieces[0].shape
    half = 32 * EDGE

    def kernel(*refs):
        mode_one_kernel(first, *refs)

    return mode_call(
        kernel,
        "mode_one_other_core" if first else "mode_one_own_core",
        order,
        [blocks] + pieces,
        [],
        [jax.ShapeDtypeStruct((half, rank), F32)]
        + ([jax.ShapeDtypeStruct((8, 128), F32)] if first else []),
        [pltpu.VMEM((4 * own, rank), BF16), pltpu.VMEM((half + EDGE, rank), F32)],
    )


def mode_two(first, order, blocks, pieces, resident):
    rank = pieces[0].shape[1]
    part = 16 * EDGE
    sent = jax.ShapeDtypeStruct((part, rank), BF16)
    if first:
        out_shape = [sent] * 3 + [jax.ShapeDtypeStruct((64 * EDGE, rank), BF16)]
    else:
        out_shape = [jax.ShapeDtypeStruct((part, rank), F32)]
    return mode_call(
        mode_two_others_kernel if first else mode_two_own_kernel,
        "mode_two_other_groups" if first else "mode_two_own_group",
        order,
        [blocks] + pieces,
        resident,
        out_shape,
        [
            pltpu.VMEM((GROUP, 8 * EDGE, 128), F32),
            pltpu.VMEM((4 * C_ROWS, rank), BF16),
            pltpu.VMEM(((3 if first else 1) * part + EDGE, rank), F32),
        ],
    )


def to_other_core(value):
    return lax.ppermute(value, "core", [(0, 1), (1, 0)])


def along_groups(value, shift):
    size = lax.axis_size("grp")
    return lax.ppermute(value, "grp", [(p, (p + shift) % size) for p in range(size)])


def exchange(value, axes):
    return lax.all_to_all(value, axes, 0, 0)


def on_device(blocks, i_index, j_index, k_index, block_count, b_factor, c_factor):
    rank = b_factor.shape[1]
    grp, core = lax.axis_index("grp"), lax.axis_index("core")
    plane = lax.axis_size(PLANE)
    chips = lax.axis_size(CHIPS)
    meta = jnp.stack([block_count[0], grp, core])

    own, gram_keep, gram_send = prepare(meta, b_factor, c_factor)
    order_one, order_two = order_slots(meta, i_index, j_index, k_index)
    pieces = [own] + [along_groups(own, q) for q in (1, 2, 3)]
    gram_pair = gram_keep + to_other_core(gram_send)
    send, ring = mode_one(True, order_one, blocks, pieces)
    gram_pair, send, pieces = lax.optimization_barrier((gram_pair, send, pieces))
    gram_parts = exchange(gram_pair.reshape(chips, -1, 8, 128), CHIPS)
    [keep] = mode_one(False, order_one, blocks, pieces)
    gram_parts, keep = lax.optimization_barrier((gram_parts, keep))
    piece = jnp.sum(gram_parts, axis=0)
    gram_near = exchange(jnp.broadcast_to(piece[None], (chips,) + piece.shape), CHIPS)
    gram_near = gram_near.reshape(-1, 8, 128)
    gram_far = to_other_core(gram_near)
    rings = (ring, to_other_core(ring))

    pair_sum = (keep + to_other_core(send)).astype(BF16)
    arrived = exchange(pair_sum.reshape(plane, -1, rank), PLANE)
    sum_own = jnp.sum(arrived.astype(F32), axis=0)
    sum_near = exchange(jnp.broadcast_to(sum_own[None], (plane,) + sum_own.shape), PLANE)
    sum_near = sum_near.reshape(-1, rank)

    inverse = inverse_of(first_inverse_kernel, "first_inverse", meta, *rings, gram_near, gram_far)
    inverse, sum_near = lax.optimization_barrier((inverse, sum_near))
    sum_far = to_other_core(sum_near)
    a_near, a_far, squares, gram_core, inverse = solve(
        sum_near, sum_far, inverse, to_other_core(inverse)
    )
    squares = squares + along_groups(squares, 1) + along_groups(squares, 2) + along_groups(squares, 3)
    squares = squares + to_other_core(squares)
    gram_plane = gram_core + to_other_core(gram_core)
    gram_parts = [gram_plane] + [along_groups(gram_plane, q) for q in (1, 2, 3)]

    *sends, a_table = mode_two(True, order_two, blocks, pieces, [a_near, a_far, squares])
    gram_parts, sends = lax.optimization_barrier((gram_parts, sends))
    second = inverse_of(
        second_inverse_kernel, "second_inverse", meta, *rings, *gram_parts, gram_near, gram_far
    )
    second, a_table = lax.optimization_barrier((second, a_table))
    [keep] = mode_two(False, order_two, blocks, pieces, [a_table])
    a_update = jnp.dot(sum_own, inverse, precision=HIGHEST)
    arrived = [along_groups(value, q + 1) for q, value in enumerate(sends)]
    arrived, keep, second = lax.optimization_barrier((arrived, keep, second))
    second = lax.optimization_barrier(second + to_other_core(second))
    arrived = [value.astype(F32) for value in arrived]
    own_two = keep + arrived[0] + arrived[1] + arrived[2]
    b_update = jnp.dot(own_two, second, precision=HIGHEST)
    return a_update, b_update


def solution(mesh):
    groups, columns = mesh.shape["grp"], mesh.shape["col"]
    side = round((columns // 2) ** 0.5)
    fine = Mesh(mesh.devices.reshape(groups, side, side, 2), ALL)
    row, flat = P(ALL, None), P(ALL)
    return jax.shard_map(
        on_device,
        mesh=fine,
        in_specs=(P(ALL, None, None), flat, flat, flat, flat, row, row),
        out_specs=(row, row),
        check_vma=False,
    )
```

```python
import jax
import jax.numpy as jnp
from jax import lax
from jax.experimental import pallas as pl
from jax.experimental.pallas import tpu as pltpu
from jax.sharding import Mesh
from jax.sharding import PartitionSpec as P

EDGE = 32
GROUP = 8
DEPTH = 4
B_ROWS = 16 * EDGE
C_ROWS = 4 * EDGE
COUNT_ROWS = 16
MODE_COST = pl.CostEstimate(flops=15_000_000_000, bytes_accessed=48_000_000, transcendentals=0)
LAST_PASS_COST = pl.CostEstimate(flops=2_000_000_000, bytes_accessed=6_000_000, transcendentals=0)
INVERSE_COST = pl.CostEstimate(flops=16_000_000_000, bytes_accessed=50_000_000, transcendentals=0)
VMEM_BYTES = 8 << 20
MODE_VMEM_BYTES = 48 << 20
ALL = ("grp", "x", "z", "core")
PLANE = ("x", "z")
CHIPS = ("grp", "x", "z")
F32 = jnp.float32
BF16 = jnp.bfloat16
HIGHEST = lax.Precision.HIGHEST


def invert_four(p):
    inv_det = 1.0 / (p[0][0] * p[1][1] - p[0][1] * p[0][1])
    a00, a01, a11 = p[1][1] * inv_det, -p[0][1] * inv_det, p[0][0] * inv_det
    t00 = a00 * p[0][2] + a01 * p[1][2]
    t01 = a00 * p[0][3] + a01 * p[1][3]
    t10 = a01 * p[0][2] + a11 * p[1][2]
    t11 = a01 * p[0][3] + a11 * p[1][3]
    s00 = p[2][2] - (p[0][2] * t00 + p[1][2] * t10)
    s01 = p[2][3] - (p[0][2] * t01 + p[1][2] * t11)
    s11 = p[3][3] - (p[0][3] * t01 + p[1][3] * t11)
    inv_det = 1.0 / (s00 * s11 - s01 * s01)
    z00, z01, z11 = s11 * inv_det, -s01 * inv_det, s00 * inv_det
    u00, u01 = t00 * z00 + t01 * z01, t00 * z01 + t01 * z11
    u10, u11 = t10 * z00 + t11 * z01, t10 * z01 + t11 * z11
    x00 = a00 + (u00 * t00 + u01 * t01)
    x01 = a01 + (u00 * t10 + u01 * t11)
    x11 = a11 + (u10 * t10 + u11 * t11)
    return [
        [x00, x01, -u00, -u01],
        [x01, x11, -u10, -u11],
        [-u00, -u10, z00, z01],
        [-u01, -u11, z01, z11],
    ]


def invert_block(w):
    n = w.shape[0]
    row = lax.broadcasted_iota(jnp.int32, (n, n), 0)
    col = lax.broadcasted_iota(jnp.int32, (n, n), 1)
    for k in range(0, n, 4):
        cols = [jnp.broadcast_to(w[:, k + q : k + q + 1], (n, n)) for q in range(4)]
        rows = [w[k + q : k + q + 1, :] for q in range(4)]
        pivot = [[cols[b][k + a : k + a + 1, :] for b in range(4)] for a in range(4)]
        inv = invert_four(pivot)
        lane = col[0:1, :]
        fresh = []
        for a in range(4):
            value = (inv[a][0] * rows[0] + inv[a][1] * rows[1]) + (
                inv[a][2] * rows[2] + inv[a][3] * rows[3]
            )
            for b in range(4):
                value = jnp.where(lane == k + b, inv[a][b], value)
            fresh.append(value)
        in_cols = (col >= k) & (col < k + 4)
        in_rows = (row >= k) & (row < k + 4)
        base = jnp.where(in_cols, 0.0, w)
        update = (cols[0] * fresh[0] + cols[1] * fresh[1]) + (
            cols[2] * fresh[2] + cols[3] * fresh[3]
        )
        out = base - update
        for a in range(4):
            out = jnp.where(row == k + a, fresh[a], out)
        w = out
    return w


def tiles_of(matrix):
    across = matrix.shape[1] // 128
    return [
        (r * across + c, slice(r * 8, r * 8 + 8), slice(c * 128, c * 128 + 128))
        for r in range(matrix.shape[0] // 8)
        for c in range(across)
    ]


def invert(out, work):
    n = work.shape[0]
    width = 64
    row = lax.broadcasted_iota(jnp.int32, (n, n), 0)
    col = lax.broadcasted_iota(jnp.int32, (n, n), 1)
    diag = jnp.where(row == col, work[...], 0.0)
    scale_row = lax.rsqrt(jnp.sum(diag, axis=0, keepdims=True))
    scale_col = lax.rsqrt(jnp.sum(diag, axis=1, keepdims=True))
    work[...] = work[...] * scale_row * scale_col
    for b in range(n // width):
        span = slice(b * width, (b + 1) * width)
        block = invert_block(work[span, span])
        rows = jnp.dot(block, work[span, :], precision=HIGHEST, preferred_element_type=F32)
        parts = [jnp.zeros((width, width), F32)] * (n // width)
        parts[b] = block
        padded = jnp.concatenate(parts, axis=1)
        in_block = (col >= b * width) & (col < (b + 1) * width)
        rows = jnp.where(in_block[0:width], padded, rows)
        left = work[:, span]
        left_row = row[:, 0:width]
        left = jnp.where((left_row >= b * width) & (left_row < (b + 1) * width), 0.0, left)
        base = jnp.where(in_block, 0.0, work[...])
        work[...] = base - jnp.dot(left, rows, precision=HIGHEST, preferred_element_type=F32)
        work[span, :] = rows
    out[...] = work[...] * scale_row * scale_col


def takes_turn(meta, ring, other_ring):
    mine, other = jnp.max(ring[...]), jnp.max(other_ring[...])
    return (mine < other) | ((mine == other) & (meta[2] == 0))


def first_inverse_kernel(meta, ring, other_ring, near, far, out, work):
    mine = takes_turn(meta, ring, other_ring)

    @pl.when(jnp.logical_not(mine))
    def _():
        out[...] = jnp.zeros_like(out)

    @pl.when(mine)
    def _():
        for t, rows, cols in tiles_of(work):
            work[rows, cols] = near[t] * far[t]
        invert(out, work)


def second_inverse_kernel(
    meta, ring, other_ring, part_0, part_1, part_2, part_3, near, far, out, work
):
    n = work.shape[0]
    mine = takes_turn(meta, ring, other_ring)

    @pl.when(jnp.logical_not(mine))
    def _():
        out[...] = jnp.zeros_like(out)

    @pl.when(mine)
    def _():
        gram = (part_0[...] + part_1[...]) + (part_2[...] + part_3[...])
        row = lax.broadcasted_iota(jnp.int32, (n, n), 0)
        col = lax.broadcasted_iota(jnp.int32, (n, n), 1)
        diag = jnp.where(row == col, gram, 0.0)
        norm_row = jnp.sqrt(jnp.sum(diag, axis=0, keepdims=True) + 1e-06)
        norm_col = jnp.sqrt(jnp.sum(diag, axis=1, keepdims=True) + 1e-06)
        work[...] = gram / (norm_col * norm_row)
        third_is_near = meta[2] == 1
        for t, rows, cols in tiles_of(work):
            work[rows, cols] = work[rows, cols] * jnp.where(third_is_near, near[t], far[t])
        invert(out, work)


def inverse_of(kernel, name, meta, *arrays):
    n = 256
    return pl.pallas_call(
        kernel,
        out_shape=jax.ShapeDtypeStruct((n, n), F32),
        in_specs=[pl.BlockSpec(memory_space=pltpu.SMEM)]
        + [pl.BlockSpec(memory_space=pltpu.VMEM)] * len(arrays),
        out_specs=pl.BlockSpec(memory_space=pltpu.VMEM),
        scratch_shapes=[pltpu.VMEM((n, n), F32)],
        compiler_params=pltpu.CompilerParams(vmem_limit_bytes=VMEM_BYTES),
        cost_estimate=INVERSE_COST,
        name=name,
    )(meta, *arrays)


def prepare_kernel(meta, b_hbm, c_hbm, own, gram_keep, gram_send, b_factor, c_factor, sems):
    rows = b_factor.shape[0]
    core = meta[2]
    wait_all(
        copy_all(
            [
                pltpu.make_async_copy(b_hbm, b_factor, sems.at[0]),
                pltpu.make_async_copy(c_hbm, c_factor, sems.at[1]),
            ]
        )
    )
    own[0:rows, :] = b_factor[...].astype(BF16)
    own[rows : rows + C_ROWS, :] = c_factor[...].astype(BF16)
    count = meta[0].astype(F32)
    own[rows + C_ROWS :, :] = jnp.full((COUNT_ROWS, own.shape[1]), count, F32).astype(BF16)
    for q, ref in enumerate((b_factor, c_factor)):
        gram = lax.dot_general(
            ref[...],
            ref[...],
            (((0,), (0,)), ((), ())),
            precision=HIGHEST,
            preferred_element_type=F32,
        )

        @pl.when(core == q)
        def _():
            for t, r, c in tiles_of(gram):
                gram_keep[t] = gram[r, c]

        @pl.when(core != q)
        def _():
            for t, r, c in tiles_of(gram):
                gram_send[t] = gram[r, c]


def prepare(meta, b_factor, c_factor):
    rank = b_factor.shape[1]
    rows = b_factor.shape[0] + c_factor.shape[0] + COUNT_ROWS
    tiles = jax.ShapeDtypeStruct((rank * rank // 1024, 8, 128), F32)
    return pl.pallas_call(
        prepare_kernel,
        out_shape=[jax.ShapeDtypeStruct((rows, rank), BF16), tiles, tiles],
        in_specs=[pl.BlockSpec(memory_space=pltpu.SMEM)]
        + [pl.BlockSpec(memory_space=pl.ANY)] * 2,
        scratch_shapes=[
            pltpu.VMEM(b_factor.shape, F32),
            pltpu.VMEM(c_factor.shape, F32),
            pltpu.SemaphoreType.DMA((2,)),
        ],
        compiler_params=pltpu.CompilerParams(vmem_limit_bytes=VMEM_BYTES),
        name="prepare",
    )(meta, b_factor, c_factor)


def order_kernel(meta, i_idx, j_idx, k_idx, order):
    slots = i_idx.shape[0]
    count, grp, core = meta[0], meta[1], meta[2]

    def place(s, front, i, j, k):
        other = jnp.where((j >> 4) == grp, 0, 1)
        order[jnp.where(other == 1, front, slots - 1 - (s - front))] = s + 256 * (
            i + 64 * (j + 64 * k)
        )
        return front + other

    def place_four(q, front):
        found = [(i_idx[4 * q + u], j_idx[4 * q + u], k_idx[4 * q + u]) for u in range(4)]
        for u in range(4):
            front = place(4 * q + u, front, *found[u])
        return front

    def place_one(s, front):
        return place(s, front, i_idx[s], j_idx[s], k_idx[s])

    fours = count // 4
    front = lax.fori_loop(0, fours, place_four, jnp.int32(0))
    front = lax.fori_loop(4 * fours, count, place_one, front)
    order[slots] = front
    order[slots + 1] = count - front
    order[slots + 2] = grp
    order[slots + 3] = core


def order_slots(meta, i_index, j_index, k_index):
    smem = pl.BlockSpec(memory_space=pltpu.SMEM)
    return pl.pallas_call(
        order_kernel,
        out_shape=jax.ShapeDtypeStruct((i_index.shape[0] + 64,), jnp.int32),
        in_specs=[smem] * 4,
        out_specs=smem,
        name="order_slots",
    )(meta, i_index, j_index, k_index)


def block_rows(ref, start):
    return ref[pl.ds(pl.multiple_of(start, EDGE), EDGE), :]


def copy_all(copies):
    for copy in copies:
        copy.start()
    return copies


def wait_all(copies):
    for copy in copies:
        copy.wait()


def for_each_group(part, order, blocks, buffer, sems, prepare_tables, one_slot):
    slots = blocks.shape[0]
    front, back = order[slots], order[slots + 1]
    count = {"all": front + back, "front": front, "back": back}[part]
    skipped = front if part == "all" else jnp.int32(slots if part == "front" else 0)
    groups = (count + GROUP - 1) // GROUP

    def entry_at(place):
        place = jnp.minimum(place, count - 1)
        return order[jnp.where(place < skipped, place, slots - 1 - (place - skipped))]

    def copies(group):
        side = group & (DEPTH - 1)
        return [
            pltpu.make_async_copy(
                blocks.at[entry_at(group * GROUP + u) & 255], buffer.at[side, u], sems.at[side, u]
            )
            for u in range(GROUP)
        ]

    for ahead in range(DEPTH - 1):

        @pl.when(ahead < groups)
        def _():
            copy_all(copies(ahead))

    prepare_tables()

    def one_group(group, carry):
        @pl.when(group + DEPTH - 1 < groups)
        def _():
            copy_all(copies(group + DEPTH - 1))

        wait_all(copies(group))
        for u in range(GROUP):
            place = group * GROUP + u
            entry = entry_at(place)
            i, j, k = (entry >> 8) & 63, (entry >> 14) & 63, (entry >> 20) & 15
            one_slot(buffer[group & (DEPTH - 1), u], u, i, j, k, place < count)
        return carry

    lax.fori_loop(0, groups, one_group, 0)


def mode_one_kernel(
    order, blocks, own_0, own_1, own_2, own_3, keep, send, ring, buffer, table, acc, sems, table_sems
):
    core = order[blocks.shape[0] + 3]
    grp = order[blocks.shape[0] + 2]
    own = own_0.shape[0]
    half = keep.shape[0]

    def prepare_tables():
        pieces = copy_all(
            [
                pltpu.make_async_copy(ref, table.at[pl.ds(q * own, own)], table_sems.at[q])
                for q, ref in enumerate((own_0, own_1, own_2, own_3))
            ]
        )
        acc[...] = jnp.zeros_like(acc)
        wait_all(pieces)

    def one_slot(block, u, i, j, k, live):
        b_rows = block_rows(table, ((grp - (j >> 4)) & 3) * own + (j & 15) * EDGE)
        c_rows = block_rows(table, ((grp - (k >> 2)) & 3) * own + B_ROWS + (k & 3) * EDGE)
        product = (b_rows[:, None, :] * c_rows[None, :, :]).reshape(EDGE * EDGE, -1)
        result = jnp.dot(block, product, preferred_element_type=F32)
        target = (((i >> 1) & 1) ^ core) * half + (i >> 2) * (2 * EDGE) + (i & 1) * EDGE
        target = jnp.where(live, target, 2 * half)
        acc[pl.ds(pl.multiple_of(target, EDGE), EDGE), :] += result

    for_each_group("all", order, blocks, buffer, sems, prepare_tables, one_slot)
    keep[...] = acc[0:half, :]
    send[...] = acc[half : 2 * half, :]
    counts = [
        table[(q + 1) * own - COUNT_ROWS : (q + 1) * own, 0:128].astype(F32) for q in range(4)
    ]
    most = jnp.maximum(jnp.maximum(counts[0], counts[1]), jnp.maximum(counts[2], counts[3]))
    ring[...] = most[0:8, :]


def turn_block(block, turned, u):
    lane = lax.broadcasted_iota(jnp.int32, (8, 128), 1)
    low_half = lane < 64
    even_group = (lane // 32) % 2 == 0
    wide = block.astype(F32)
    for jh in range(8):
        t = [wide[il * 8 : il * 8 + 8, jh * 128 : jh * 128 + 128] for il in range(4)]
        m = [None] * 4
        for il in range(2):
            m[il] = jnp.where(low_half, t[il], pltpu.roll(t[il + 2], 64, 1))
            m[il + 2] = jnp.where(low_half, pltpu.roll(t[il], 64, 1), t[il + 2])
        for q in (0, 2):
            j = jh * 4 + q
            turned[u, j * 8 : j * 8 + 8, :] = jnp.where(
                even_group, m[q], pltpu.roll(m[q + 1], 32, 1)
            )
            turned[u, j * 8 + 8 : j * 8 + 16, :] = jnp.where(
                even_group, pltpu.roll(m[q], 96, 1), m[q + 1]
            )
    return jnp.concatenate(
        [turned[u, pl.ds(ih, EDGE, stride=8), :].astype(BF16) for ih in range(8)], axis=1
    )


def mode_two_slots(first, order, blocks, owns, a_table, scratch, part):
    buffer, turned, table, acc, sems, table_sems = scratch
    grp, core = order[blocks.shape[0] + 2], order[blocks.shape[0] + 3]
    half = a_table.shape[0] // 2

    def prepare_tables():
        pieces = copy_all(
            [
                pltpu.make_async_copy(
                    ref.at[pl.ds(B_ROWS, C_ROWS)],
                    table.at[pl.ds(q * C_ROWS, C_ROWS)],
                    table_sems.at[q],
                )
                for q, ref in enumerate(owns)
            ]
        )
        acc[...] = jnp.zeros_like(acc)
        wait_all(pieces)

    def one_slot(block, u, i, j, k, live):
        a_rows = block_rows(
            a_table,
            (((i >> 1) & 1) ^ core) * half + (i >> 2) * (2 * EDGE) + (i & 1) * EDGE,
        )
        c_rows = block_rows(table, ((grp - (k >> 2)) & 3) * C_ROWS + (k & 3) * EDGE)
        left = turn_block(block, turned, u)
        product = jnp.concatenate(
            [
                a_rows[il * 8 + ih : il * 8 + ih + 1, :] * c_rows
                for ih in range(8)
                for il in range(4)
            ],
            axis=0,
        )
        result = jnp.dot(left, product, preferred_element_type=F32)
        target = (j & 15) * EDGE
        if first:
            target += (((j >> 4) - grp - 1) & 3) * part
        target = jnp.where(live, target, acc.shape[0] - EDGE)
        acc[pl.ds(pl.multiple_of(target, EDGE), EDGE), :] += result

    part_of = "front" if first else "back"
    for_each_group(part_of, order, blocks, buffer, sems, prepare_tables, one_slot)


def mode_two_others_kernel(
    order,
    blocks,
    own_0,
    own_1,
    own_2,
    own_3,
    a_near,
    a_far,
    squares,
    send_1,
    send_2,
    send_3,
    a_table,
    *scratch,
):
    half = a_near.shape[0]
    part = send_1.shape[0]
    inv_norm = 1.0 / jnp.sqrt(squares[...] + 1e-06)
    a_table[0:half, :] = (a_near[...] * inv_norm).astype(BF16)
    a_table[half : 2 * half, :] = (a_far[...] * inv_norm).astype(BF16)
    mode_two_slots(True, order, blocks, (own_0, own_1, own_2, own_3), a_table, scratch, part)
    acc = scratch[3]
    for q, ref in enumerate((send_1, send_2, send_3)):
        ref[...] = acc[q * part : (q + 1) * part, :].astype(BF16)


def mode_two_own_kernel(order, blocks, own_0, own_1, own_2, own_3, a_table, keep, *scratch):
    part = keep.shape[0]
    mode_two_slots(False, order, blocks, (own_0, own_1, own_2, own_3), a_table, scratch, part)
    keep[...] = scratch[3][0:part, :]


def mode_call(kernel, name, order, in_place, resident, out_shape, scratch):
    smem, anywhere, vmem = (
        pl.BlockSpec(memory_space=pltpu.SMEM),
        pl.BlockSpec(memory_space=pl.ANY),
        pl.BlockSpec(memory_space=pltpu.VMEM),
    )
    blocks = in_place[0]
    buffer = pltpu.VMEM((DEPTH, GROUP) + blocks.shape[1:], blocks.dtype)
    return pl.pallas_call(
        kernel,
        out_shape=out_shape,
        in_specs=[smem] + [anywhere] * len(in_place) + [vmem] * len(resident),
        out_specs=[vmem] * len(out_shape),
        scratch_shapes=[buffer]
        + scratch
        + [pltpu.SemaphoreType.DMA((DEPTH, GROUP)), pltpu.SemaphoreType.DMA((4,))],
        compiler_params=pltpu.CompilerParams(vmem_limit_bytes=MODE_VMEM_BYTES),
        cost_estimate=LAST_PASS_COST if name == "mode_two_own_group" else MODE_COST,
        name=name,
    )(order, *in_place, *resident)


def mode_one(order, blocks, pieces):
    own, rank = pieces[0].shape
    half = 32 * EDGE
    return mode_call(
        mode_one_kernel,
        "mode_one",
        order,
        [blocks] + pieces,
        [],
        [jax.ShapeDtypeStruct((half, rank), F32)] * 2 + [jax.ShapeDtypeStruct((8, 128), F32)],
        [pltpu.VMEM((4 * own, rank), BF16), pltpu.VMEM((2 * half + EDGE, rank), F32)],
    )


def mode_two(first, order, blocks, pieces, resident):
    rank = pieces[0].shape[1]
    part = 16 * EDGE
    sent = jax.ShapeDtypeStruct((part, rank), BF16)
    if first:
        out_shape = [sent] * 3 + [jax.ShapeDtypeStruct((64 * EDGE, rank), BF16)]
    else:
        out_shape = [jax.ShapeDtypeStruct((part, rank), F32)]
    return mode_call(
        mode_two_others_kernel if first else mode_two_own_kernel,
        "mode_two_other_groups" if first else "mode_two_own_group",
        order,
        [blocks] + pieces,
        resident,
        out_shape,
        [
            pltpu.VMEM((GROUP, 8 * EDGE, 128), F32),
            pltpu.VMEM((4 * C_ROWS, rank), BF16),
            pltpu.VMEM(((3 if first else 1) * part + EDGE, rank), F32),
        ],
    )


def to_other_core(value):
    return lax.ppermute(value, "core", [(0, 1), (1, 0)])


def along_groups(value, shift):
    size = lax.axis_size("grp")
    return lax.ppermute(value, "grp", [(p, (p + shift) % size) for p in range(size)])


def exchange(value, axes):
    return lax.all_to_all(value, axes, 0, 0)


def on_device(blocks, i_index, j_index, k_index, block_count, b_factor, c_factor):
    rank = b_factor.shape[1]
    grp, core = lax.axis_index("grp"), lax.axis_index("core")
    plane = lax.axis_size(PLANE)
    chips = lax.axis_size(CHIPS)
    meta = jnp.stack([block_count[0], grp, core])

    own, gram_keep, gram_send = prepare(meta, b_factor, c_factor)
    gram_pair = gram_keep + to_other_core(gram_send)
    gram_pair, late_meta = lax.optimization_barrier((gram_pair, meta))
    order = order_slots(late_meta, i_index, j_index, k_index)
    pieces = [own] + [along_groups(own, q) for q in (1, 2, 3)]
    piece = jnp.sum(exchange(gram_pair.reshape(chips, -1, 8, 128), CHIPS), axis=0)
    spread = jnp.broadcast_to(piece[None], (chips,) + piece.shape)
    spread, order = lax.optimization_barrier((spread, order))
    gram_near = exchange(spread, CHIPS)
    keep, send, ring = mode_one(order, blocks, pieces)
    gram_near, keep, send = lax.optimization_barrier((gram_near, keep, send))
    gram_near = gram_near.reshape(-1, 8, 128)
    gram_far = to_other_core(gram_near)
    rings = (ring, to_other_core(ring))

    pair_sum = (keep + to_other_core(send)).astype(BF16)
    arrived = exchange(pair_sum.reshape(plane, -1, rank), PLANE)
    sum_own = jnp.sum(arrived.astype(F32), axis=0)
    sum_near = exchange(jnp.broadcast_to(sum_own[None], (plane,) + sum_own.shape), PLANE)
    sum_near = sum_near.reshape(-1, rank)

    inverse = inverse_of(first_inverse_kernel, "first_inverse", meta, *rings, gram_near, gram_far)
    inverse = lax.optimization_barrier(inverse + to_other_core(inverse))

    sum_far = to_other_core(sum_near)
    a_near = jnp.dot(sum_near, inverse, precision=HIGHEST)
    squares = jnp.sum(a_near * a_near, axis=0, keepdims=True)
    squares = squares + along_groups(squares, 1) + along_groups(squares, 2) + along_groups(squares, 3)
    squares = squares + to_other_core(squares)
    a_far = jnp.dot(sum_far, inverse, precision=HIGHEST)
    gram_core = jnp.dot(a_near.T, a_near, precision=HIGHEST)
    gram_plane = gram_core + to_other_core(gram_core)
    gram_parts = [gram_plane] + [along_groups(gram_plane, q) for q in (1, 2, 3)]

    *sends, a_table = mode_two(True, order, blocks, pieces, [a_near, a_far, squares])
    gram_parts, sends = lax.optimization_barrier((gram_parts, sends))
    second = inverse_of(
        second_inverse_kernel, "second_inverse", meta, *rings, *gram_parts, gram_near, gram_far
    )
    second, a_table = lax.optimization_barrier((second, a_table))
    [keep] = mode_two(False, order, blocks, pieces, [a_table])
    a_update = jnp.dot(sum_own, inverse, precision=HIGHEST)
    arrived = [along_groups(value, q + 1) for q, value in enumerate(sends)]
    arrived, keep, second = lax.optimization_barrier((arrived, keep, second))
    second = lax.optimization_barrier(second + to_other_core(second))
    arrived = [value.astype(F32) for value in arrived]
    own_two = keep + arrived[0] + arrived[1] + arrived[2]
    b_update = jnp.dot(own_two, second, precision=HIGHEST)
    return a_update, b_update


def solution(mesh):
    groups, columns = mesh.shape["grp"], mesh.shape["col"]
    side = round((columns // 2) ** 0.5)
    fine = Mesh(mesh.devices.reshape(groups, side, side, 2), ALL)
    row, flat = P(ALL, None), P(ALL)
    return jax.shard_map(
        on_device,
        mesh=fine,
        in_specs=(P(ALL, None, None), flat, flat, flat, flat, row, row),
        out_specs=(row, row),
        check_vma=False,
    )
```
